32 devices in a mesh: groups: 1, freq: 32 (over z, y, x, core).
Axes of the slice: x: 2, y: 2, z: 4, core: 2. Of those that a mesh axis runs over, the one named last changes fastest.
Arguments:
- mag_field: float32 [2, 256, 16384], P(None, 'groups', 'freq'), may hold values from -6 to 6
- node_order: int32 [256], P('groups'), may hold values from 0 to 255, each once
- source_blocks: int32 [4, 4], P('groups'), may hold values from 0 to 3
- impedance: float32 [4, 8, 4, 8192], P(None, None, 'groups', 'freq'), may hold values from -4 to 4
Outputs:
- electric_field: float32 [2, 256, 16384], P(None, 'groups', 'freq')
The draws below stay inside these ranges and needn't reach their ends.
Inputs may be any that keep to these rules, and one draw needn't show every extreme that they name: node_order holds every node exactly once. `source_blocks`: block numbers; a block may be listed more than once.
All inputs are finite; a program needn't handle non-finite values.
Results may differ from the reference program's by a relative error of at most 0.00007.
Values sent between devices are 32-bit elements; how exact they have to be, the bound alone decides.
No kernel may reach another device: no remote copies, remote signals or barrier semaphores. Data moves between devices by JAX's collectives and lax.ppermute only.
A program may use at most 64 MiB of HBM per device.

```python
import jax
import jax.numpy as jnp
from jax import lax

NT = 16384
HALF_SPECTRUM = 8192
NODES = 256
BSIZE = 64
BLOCKS = 4
NBR = 4


def place_ends(array, stream_key, smallest, largest):
    spot = [jax.random.randint(jax.random.fold_in(stream_key, axis), (), 0, length) for axis, length in enumerate(array.shape)]
    main_axis = array.shape.index(max(array.shape))
    next_to = spot[:main_axis] + [(spot[main_axis] + 1) % array.shape[main_axis]] + spot[main_axis + 1:]
    return array.at[tuple(spot)].set(smallest).at[tuple(next_to)].set(largest)


def level_of(own_key, dims, pieces, low, largest):
    def one(axis_at, blocks):
        heights = jax.random.uniform(jax.random.fold_in(jax.random.fold_in(own_key, 6), axis_at), (blocks,), jnp.float32, low / len(pieces), largest / len(pieces))
        return jnp.repeat(jnp.exp(heights), dims[axis_at] // blocks).reshape((-1,) + (1,) * (len(dims) - axis_at - 1))

    factor_of = one(*pieces[0])
    for cut in pieces[1:]:
        factor_of = factor_of * one(*cut)
    return factor_of


def normal_values(key, extent, deviation, reach, split=(), held_as=jnp.bfloat16):
    values = deviation * jax.random.normal(key, extent, jnp.float32)
    if split:
        values = values * level_of(key, extent, split, -0.22, 0.18)
    return jnp.clip(values, -reach, reach).astype(held_as)


def setup_inputs(seed: int = 0, part: int = 0) -> dict:
    streams_of = jax.random.split(jax.random.key(seed), 5)
    own_keys = jax.random.split(jax.random.fold_in(streams_of[4], part), 5)
    return {
        "mag_field": normal_values(own_keys[0], (2, NODES, NT), 1.0, 6.0, ((2, 32),), jnp.float32),
        "node_order": jax.random.permutation(own_keys[1], NODES).astype(jnp.int32),
        "source_blocks": place_ends(jax.random.randint(own_keys[2], (BLOCKS, NBR), 0, BLOCKS), jax.random.fold_in(own_keys[2], 1), 0, BLOCKS - 1).astype(jnp.int32),
        "impedance": normal_values(own_keys[3], (NBR, 8, BLOCKS, HALF_SPECTRUM), 0.5, 4.0, ((3, 32),), jnp.float32),
    }


def reference(mag_field, node_order, source_blocks, impedance):
    spectrum = jnp.fft.fft(lax.complex(mag_field[0], mag_field[1]), axis=-1)
    positive = spectrum[:, :HALF_SPECTRUM]
    mirrored = jnp.concatenate([spectrum[:, :1], spectrum[:, :HALF_SPECTRUM:-1]], axis=1)
    bx_hat = (positive + jnp.conj(mirrored)) * 0.5
    by_hat = (positive - jnp.conj(mirrored)) * (-0.5j)
    slots = node_order.reshape(BLOCKS, BSIZE)
    tensors = lax.complex(impedance[:, 0::2], impedance[:, 1::2])
    ex_block = jnp.zeros((BLOCKS, BSIZE, HALF_SPECTRUM), spectrum.dtype)
    ey_block = jnp.zeros((BLOCKS, BSIZE, HALF_SPECTRUM), spectrum.dtype)
    for source in range(NBR):
        nodes_src = slots[source_blocks[:, source]]
        bx_src = bx_hat[nodes_src]
        by_src = by_hat[nodes_src]
        ex_block = ex_block + tensors[source, 0][:, None, :] * bx_src + tensors[source, 1][:, None, :] * by_src
        ey_block = ey_block + tensors[source, 2][:, None, :] * bx_src + tensors[source, 3][:, None, :] * by_src
    keep = (jnp.arange(HALF_SPECTRUM) > 0)[None, None, :]
    ex_block = jnp.where(keep, ex_block, jnp.zeros_like(ex_block))
    ey_block = jnp.where(keep, ey_block, jnp.zeros_like(ey_block))
    east_field_nodes = jnp.zeros((NODES, HALF_SPECTRUM), spectrum.dtype).at[node_order].set(ex_block.reshape(NODES, HALF_SPECTRUM))
    north_field_nodes = jnp.zeros((NODES, HALF_SPECTRUM), spectrum.dtype).at[node_order].set(ey_block.reshape(NODES, HALF_SPECTRUM))
    packed_upper = east_field_nodes + 1j * north_field_nodes
    packed_reflected = jnp.conj(east_field_nodes) + 1j * jnp.conj(north_field_nodes)
    packed_spectrum = jnp.concatenate([packed_upper, jnp.zeros_like(packed_upper[:, :1]), packed_reflected[:, :0:-1]], axis=1)
    series = jnp.fft.ifft(packed_spectrum, axis=-1)
    return jnp.stack([jnp.real(series), jnp.imag(series)])
```

```python
import functools
import math

import jax
import jax.numpy as jnp
import ml_dtypes
import numpy as np
from jax import lax
from jax.experimental import pallas as pl
from jax.experimental.pallas import tpu as pltpu
from jax.sharding import PartitionSpec as P

RADIX = 128
HALF_RADIX = 64
NT = 16384
BSIZE = 64
NBR = 4
VMEM_SPACE = pl.BlockSpec(memory_space=pltpu.VMEM)
SMEM_SPACE = pl.BlockSpec(memory_space=pltpu.SMEM)


def halves(table):
    high = table.astype(ml_dtypes.bfloat16)
    low = (table - high.astype(np.float64)).astype(ml_dtypes.bfloat16)
    return high, low


def wide(table):
    high, low = halves(table)
    return np.concatenate([high, low, high], axis=1)


@functools.cache
def tables():
    full = np.arange(RADIX)
    half = np.arange(HALF_RADIX)

    def wave(rows, cols, modulus):
        theta = 2.0 * math.pi / modulus * (np.outer(rows, cols) % modulus)
        return np.cos(theta), np.sin(theta)

    cos1, sin1 = wave(full, full, RADIX)
    first = np.concatenate([cos1, -sin1], axis=0)
    cos2, sin2 = wave(half, full, RADIX)
    second = np.block([[cos2, sin2], [-sin2, cos2]])
    third = np.block([[cos2.T, -sin2.T], [sin2.T, cos2.T]])
    fourth = np.concatenate([cos1, -sin1], axis=1) * (2.0 / NT)
    twist_cos, twist_sin = wave(full, full, NT)
    return (
        wide(first),
        wide(second),
        wide(third),
        wide(fourth),
        twist_cos.astype(np.float32),
        twist_sin.astype(np.float32),
    )


def two_terms(x):
    high = x.astype(jnp.bfloat16)
    return high, (x - high.astype(jnp.float32)).astype(jnp.bfloat16)


def three_terms(x):
    high = x.astype(jnp.bfloat16)
    rest = x - high.astype(jnp.float32)
    middle = rest.astype(jnp.bfloat16)
    return high, middle, (rest - middle.astype(jnp.float32)).astype(jnp.bfloat16)


def dot_plain(table, x):
    high, low = two_terms(x)
    return jnp.dot(
        table, jnp.concatenate([high, high, low], axis=0), preferred_element_type=jnp.float32
    )


def dot_turned(table, x):
    high, low = two_terms(x)
    return lax.dot_general(
        table,
        jnp.concatenate([high, high, low], axis=1),
        (((1,), (1,)), ((), ())),
        preferred_element_type=jnp.float32,
    )


def slot_of_row(place, blocks, slots, slot):
    device, block = place // (2 * blocks), place % blocks
    return block * BSIZE + device * slots + slot


def gather_kernel(blocks, slots, slot, order_ref, mag_ref, out_ref):
    devices, parts, series, _ = out_ref.shape
    rows, total = devices * series, order_ref.shape[1]
    row = lax.broadcasted_iota(jnp.int32, (rows, 1), 0)
    wanted = slot_of_row(row, blocks, slots, slot)
    lane = lax.broadcasted_iota(jnp.int32, (rows, total), 1)
    node = jnp.sum(
        jnp.where(lane == wanted, order_ref[...], 0).astype(jnp.float32), axis=1, keepdims=True
    ).astype(jnp.int32)
    source = node + (row // blocks) % 2 * total
    lane = lax.broadcasted_iota(jnp.int32, (rows, 2 * total), 1)
    pick = jnp.where(lane == source, 1.0, 0.0).astype(jnp.bfloat16)
    picked = sum(
        jnp.dot(pick, term, preferred_element_type=jnp.float32) for term in three_terms(mag_ref[...])
    )
    for part in range(parts):
        out_ref[:, part] = picked[:, part * RADIX : (part + 1) * RADIX].reshape(devices, series, RADIX)


def scatter_kernel(blocks, slots, order_ref, *refs):
    *in_refs, out_ref = refs
    devices, parts, series, _ = in_refs[0].shape
    rows, total = devices * series, order_ref.shape[0]
    column = lax.broadcasted_iota(jnp.int32, (1, rows), 1)
    place = lax.broadcasted_iota(jnp.int32, (total, rows), 0)
    target = lax.broadcasted_iota(jnp.int32, (2 * total, rows), 0)
    placed = 0.0
    for slot, in_ref in enumerate(in_refs):
        wanted = slot_of_row(column, blocks, slots, slot)
        node = jnp.sum(
            jnp.where(place == wanted, order_ref[...], 0).astype(jnp.float32), axis=0, keepdims=True
        ).astype(jnp.int32)
        node = node + (column // blocks) % 2 * total
        put = jnp.where(target == node, 1.0, 0.0).astype(jnp.bfloat16)
        value = jnp.concatenate(
            [in_ref[:, part].reshape(rows, RADIX) for part in range(parts)], axis=1
        )
        for term in three_terms(value):
            placed = placed + jnp.dot(put, term, preferred_element_type=jnp.float32)
    out_ref[...] = placed


def field_kernel(
    blocks, sources_ref, x_ref, z_ref, t1_ref, t2_ref, t3_ref, t4_ref, cos_ref, sin_ref, out_ref, spec_ref, e_ref
):
    series = 2 * blocks
    rows = NBR * 8 * blocks
    cosine, sine = cos_ref[...], sin_ref[...]
    cosine2 = jnp.concatenate([cosine, cosine], axis=1)
    sine2 = jnp.concatenate([sine, sine], axis=1)
    for block in range(blocks):
        x = jnp.concatenate(
            [x_ref[pl.ds(c * blocks + block, RADIX, stride=series), :] for c in range(2)], axis=1
        )
        y = dot_plain(t1_ref[...], x)
        y_re, y_im = y[:RADIX], y[RADIX:]
        z_re = y_re * cosine2 + y_im * sine2
        z_im = y_im * cosine2 - y_re * sine2
        z = jnp.concatenate(
            [
                jnp.concatenate([z_re[:, :RADIX], z_im[:, :RADIX]], axis=1),
                jnp.concatenate([z_re[:, RADIX:], z_im[:, RADIX:]], axis=1),
            ],
            axis=0,
        )
        spec_ref[block] = dot_turned(t2_ref[...], z)
    first = (lax.broadcasted_iota(jnp.int32, (8, RADIX), 0) == 0) & (
        lax.broadcasted_iota(jnp.int32, (8, RADIX), 1) == 0
    )
    for block in range(blocks):
        for group in range(HALF_RADIX // 8):
            ex_re = ex_im = ey_re = ey_im = 0.0
            for source in range(NBR):
                origin = sources_ref[block, source]
                re_rows = pl.ds(group * 8, 8)
                im_rows = pl.ds(HALF_RADIX + group * 8, 8)
                bx_re = spec_ref[origin, re_rows, :RADIX]
                by_re = spec_ref[origin, re_rows, RADIX:]
                bx_im = spec_ref[origin, im_rows, :RADIX]
                by_im = spec_ref[origin, im_rows, RADIX:]
                t = [
                    z_ref[pl.ds(group * 8 * rows + (source * 8 + i) * blocks + block, 8, stride=rows), :]
                    for i in range(8)
                ]
                ex_re = ex_re + (t[0] * bx_re - t[1] * bx_im) + (t[2] * by_re - t[3] * by_im)
                ex_im = ex_im + (t[0] * bx_im + t[1] * bx_re) + (t[2] * by_im + t[3] * by_re)
                ey_re = ey_re + (t[4] * bx_re - t[5] * bx_im) + (t[6] * by_re - t[7] * by_im)
                ey_im = ey_im + (t[4] * bx_im + t[5] * bx_re) + (t[6] * by_im + t[7] * by_re)
            values = [ex_re, ey_re, ex_im, ey_im]
            if group == 0:
                values = [jnp.where(first, 0.0, value) for value in values]
            e_ref[block, pl.ds(group * 8, 8), :RADIX] = values[0]
            e_ref[block, pl.ds(group * 8, 8), RADIX:] = values[1]
            e_ref[block, pl.ds(HALF_RADIX + group * 8, 8), :RADIX] = values[2]
            e_ref[block, pl.ds(HALF_RADIX + group * 8, 8), RADIX:] = values[3]
    for block in range(blocks):
        g = dot_plain(t3_ref[...], e_ref[block])
        g_re, g_im = g[:RADIX], g[RADIX:]
        h_re = g_re * cosine2 - g_im * sine2
        h_im = g_im * cosine2 + g_re * sine2
        h = jnp.concatenate(
            [
                jnp.concatenate([h_re[:, :RADIX], h_im[:, :RADIX]], axis=1),
                jnp.concatenate([h_re[:, RADIX:], h_im[:, RADIX:]], axis=1),
            ],
            axis=0,
        )
        series_out = dot_turned(t4_ref[...], h)
        for c in range(2):
            out_ref[pl.ds(c * blocks + block, RADIX, stride=series), :] = series_out[
                :, c * RADIX : (c + 1) * RADIX
            ]


def local(mag_field, node_order, source_blocks, impedance):
    devices = lax.axis_size("freq")
    total = node_order.shape[0]
    blocks = total // BSIZE
    slots = BSIZE // devices
    span = mag_field.shape[2]
    parts = span // RADIX
    series = 2 * blocks
    rows = NBR * 8 * blocks
    block_shape = (devices, parts, series, RADIX)
    limit = pltpu.CompilerParams(vmem_limit_bytes=48 << 20)

    spread = impedance.reshape(rows, -1, RADIX).transpose(1, 0, 2)
    tensors = lax.all_gather(spread, "freq", axis=0, tiled=True).reshape(HALF_RADIX * rows, RADIX)

    mag_rows = mag_field.reshape(2 * total, span)
    order_row = node_order.reshape(1, total)
    order_column = node_order.reshape(total, 1)
    constants = [jnp.asarray(table) for table in tables()]
    returned = []
    for slot in range(slots):
        outgoing = pl.pallas_call(
            functools.partial(gather_kernel, blocks, slots, slot),
            out_shape=jax.ShapeDtypeStruct(block_shape, jnp.float32),
            in_specs=[VMEM_SPACE] * 2,
            out_specs=VMEM_SPACE,
            compiler_params=limit,
            name="gather_nodes",
        )(order_row, mag_rows)
        arrived = lax.all_to_all(outgoing, "freq", split_axis=0, concat_axis=0, tiled=True)
        field = pl.pallas_call(
            functools.partial(field_kernel, blocks),
            out_shape=jax.ShapeDtypeStruct((RADIX * series, RADIX), jnp.float32),
            in_specs=[SMEM_SPACE] + [VMEM_SPACE] * 8,
            out_specs=VMEM_SPACE,
            scratch_shapes=[
                pltpu.VMEM((blocks, RADIX, 2 * RADIX), jnp.float32),
                pltpu.VMEM((blocks, RADIX, 2 * RADIX), jnp.float32),
            ],
            compiler_params=limit,
            name="field",
        )(source_blocks, arrived.reshape(RADIX * series, RADIX), tensors, *constants)
        returned.append(
            lax.all_to_all(
                field.reshape(block_shape), "freq", split_axis=0, concat_axis=0, tiled=True
            )
        )
    placed = pl.pallas_call(
        functools.partial(scatter_kernel, blocks, slots),
        out_shape=jax.ShapeDtypeStruct((2 * total, span), jnp.float32),
        in_specs=[VMEM_SPACE] * (1 + slots),
        out_specs=VMEM_SPACE,
        compiler_params=limit,
        name="scatter_nodes",
    )(order_column, *returned)
    return placed.reshape(2, total, span)


def solution(mesh):
    placed = (
        P(None, "groups", "freq"),
        P("groups"),
        P("groups", None),
        P(None, None, "groups", "freq"),
    )
    return jax.shard_map(
        local, mesh=mesh, in_specs=placed, out_specs=P(None, "groups", "freq"), check_vma=False
    )
```

```python
import functools
import math

import jax
import jax.numpy as jnp
import ml_dtypes
import numpy as np
from jax import lax
from jax.experimental import pallas as pl
from jax.experimental.pallas import tpu as pltpu
from jax.sharding import PartitionSpec as P

RADIX = 128
HALF_RADIX = 64
NT = 16384
BSIZE = 64
NBR = 4
VMEM_SPACE = pl.BlockSpec(memory_space=pltpu.VMEM)
SMEM_SPACE = pl.BlockSpec(memory_space=pltpu.SMEM)


def halves(table):
    high = table.astype(ml_dtypes.bfloat16)
    low = (table - high.astype(np.float64)).astype(ml_dtypes.bfloat16)
    return high, low


def wide(table):
    high, low = halves(table)
    return np.concatenate([high, low, high], axis=1)


@functools.cache
def tables():
    full = np.arange(RADIX)
    half = np.arange(HALF_RADIX)

    def wave(rows, cols, modulus):
        theta = 2.0 * math.pi / modulus * (np.outer(rows, cols) % modulus)
        return np.cos(theta), np.sin(theta)

    cos1, sin1 = wave(full, full, RADIX)
    first = np.concatenate([cos1, -sin1], axis=0)
    cos2, sin2 = wave(half, full, RADIX)
    second = np.block([[cos2, sin2], [-sin2, cos2]])
    third = np.block([[cos2.T, -sin2.T], [sin2.T, cos2.T]])
    fourth = np.concatenate([cos1, -sin1], axis=1) * (2.0 / NT)
    twist_cos, twist_sin = wave(full, full, NT)
    return (
        wide(first),
        wide(second),
        wide(third),
        wide(fourth),
        twist_cos.astype(np.float32),
        twist_sin.astype(np.float32),
    )


def two_terms(x):
    high = x.astype(jnp.bfloat16)
    return high, (x - high.astype(jnp.float32)).astype(jnp.bfloat16)


def three_terms(x):
    high = x.astype(jnp.bfloat16)
    rest = x - high.astype(jnp.float32)
    middle = rest.astype(jnp.bfloat16)
    return high, middle, (rest - middle.astype(jnp.float32)).astype(jnp.bfloat16)


def dot_plain(table, x):
    high, low = two_terms(x)
    return jnp.dot(
        table, jnp.concatenate([high, high, low], axis=0), preferred_element_type=jnp.float32
    )


def dot_turned(table, x):
    high, low = two_terms(x)
    return lax.dot_general(
        table,
        jnp.concatenate([high, high, low], axis=1),
        (((1,), (1,)), ((), ())),
        preferred_element_type=jnp.float32,
    )


def slot_of_row(place, blocks, slots):
    device, slot, block = place // (slots * blocks), place // blocks % slots, place % blocks
    return block * BSIZE + device * slots + slot


def gather_kernel(blocks, slots, order_ref, mag_ref, out_ref):
    devices, parts, series, _ = out_ref.shape
    total = order_ref.shape[1]
    nodes = series // 2
    row = lax.broadcasted_iota(jnp.int32, (total, 1), 0)
    wanted = slot_of_row(row, blocks, slots)
    lane = lax.broadcasted_iota(jnp.int32, (total, total), 1)
    node = jnp.sum(
        jnp.where(lane == wanted, order_ref[...], 0).astype(jnp.float32), axis=1, keepdims=True
    ).astype(jnp.int32)
    pick = jnp.where(lane == node, 1.0, 0.0).astype(jnp.bfloat16)
    for c in range(2):
        picked = sum(
            jnp.dot(pick, term, preferred_element_type=jnp.float32)
            for term in three_terms(mag_ref[c])
        )
        for part in range(parts):
            out_ref[:, part, pl.ds(c * nodes, nodes)] = picked[
                :, part * RADIX : (part + 1) * RADIX
            ].reshape(devices, nodes, RADIX)


def scatter_kernel(blocks, slots, order_ref, in_ref, out_ref):
    devices, parts, series, _ = in_ref.shape
    total = order_ref.shape[0]
    nodes = series // 2
    column = lax.broadcasted_iota(jnp.int32, (1, total), 1)
    wanted = slot_of_row(column, blocks, slots)
    place = lax.broadcasted_iota(jnp.int32, (total, total), 0)
    node = jnp.sum(
        jnp.where(place == wanted, order_ref[...], 0).astype(jnp.float32), axis=0, keepdims=True
    ).astype(jnp.int32)
    put = jnp.where(place == node, 1.0, 0.0).astype(jnp.bfloat16)
    for c in range(2):
        value = jnp.concatenate(
            [
                in_ref[:, part, pl.ds(c * nodes, nodes)].reshape(total, RADIX)
                for part in range(parts)
            ],
            axis=1,
        )
        out_ref[c] = sum(
            jnp.dot(put, term, preferred_element_type=jnp.float32) for term in three_terms(value)
        )


def turn(re, im):
    return jnp.concatenate(
        [
            jnp.concatenate([re[:, :RADIX], im[:, :RADIX]], axis=1),
            jnp.concatenate([re[:, RADIX:], im[:, RADIX:]], axis=1),
        ],
        axis=0,
    )


def forward_kernel(x_ref, first_ref, second_ref, cos_ref, sin_ref, spec_ref):
    nodes = spec_ref.shape[0]
    cosine = jnp.concatenate([cos_ref[...]] * 2, axis=1)
    sine = jnp.concatenate([sin_ref[...]] * 2, axis=1)
    for node in range(nodes):
        x = jnp.concatenate(
            [x_ref[pl.ds(c * nodes + node, RADIX, stride=2 * nodes), :] for c in range(2)], axis=1
        )
        y = dot_plain(first_ref[...], x)
        re, im = y[:RADIX], y[RADIX:]
        spec_ref[node] = dot_turned(
            second_ref[...], turn(re * cosine + im * sine, im * cosine - re * sine)
        )


def field_kernel(blocks, home, sources_ref, spec_ref, third_ref, fourth_ref, cos_ref, sin_ref, *refs):
    *piece_refs, out_ref, z_ref, e_ref, sems = refs
    nodes = spec_ref.shape[0]
    slots = nodes // blocks
    copies = []
    for piece_ref, starts in zip(piece_refs, home()):
        length = piece_ref.shape[0] // len(starts)
        for i, start in enumerate(starts):
            copy = pltpu.make_async_copy(
                piece_ref.at[pl.ds(i * length, length)],
                z_ref.at[pl.ds(start, length)],
                sems.at[len(copies)],
            )
            copy.start()
            copies.append(copy)
    for copy in copies:
        copy.wait()
    rows = z_ref.shape[1]
    flat = z_ref.reshape(HALF_RADIX * rows, RADIX)
    first = (lax.broadcasted_iota(jnp.int32, (8, RADIX), 0) == 0) & (
        lax.broadcasted_iota(jnp.int32, (8, RADIX), 1) == 0
    )
    for block in range(blocks):
        for group in range(HALF_RADIX // 8):
            re_rows = pl.ds(group * 8, 8)
            im_rows = pl.ds(HALF_RADIX + group * 8, 8)
            sums = [[0.0] * 4 for _ in range(slots)]
            for source in range(NBR):
                origin = sources_ref[block, source]
                t = [
                    flat[pl.ds(group * 8 * rows + (source * 8 + i) * blocks + block, 8, stride=rows), :]
                    for i in range(8)
                ]
                for slot in range(slots):
                    node = slot * blocks + origin
                    bx_re = spec_ref[node, re_rows, :RADIX]
                    by_re = spec_ref[node, re_rows, RADIX:]
                    bx_im = spec_ref[node, im_rows, :RADIX]
                    by_im = spec_ref[node, im_rows, RADIX:]
                    terms = [
                        (t[0] * bx_re - t[1] * bx_im) + (t[2] * by_re - t[3] * by_im),
                        (t[4] * bx_re - t[5] * bx_im) + (t[6] * by_re - t[7] * by_im),
                        (t[0] * bx_im + t[1] * bx_re) + (t[2] * by_im + t[3] * by_re),
                        (t[4] * bx_im + t[5] * bx_re) + (t[6] * by_im + t[7] * by_re),
                    ]
                    sums[slot] = [a + b for a, b in zip(sums[slot], terms)]
            for slot in range(slots):
                node = slot * blocks + block
                values = sums[slot]
                if group == 0:
                    values = [jnp.where(first, 0.0, value) for value in values]
                e_ref[node, re_rows, :RADIX] = values[0]
                e_ref[node, re_rows, RADIX:] = values[1]
                e_ref[node, im_rows, :RADIX] = values[2]
                e_ref[node, im_rows, RADIX:] = values[3]
    cosine = jnp.concatenate([cos_ref[...]] * 2, axis=1)
    sine = jnp.concatenate([sin_ref[...]] * 2, axis=1)
    for node in range(nodes):
        g = dot_plain(third_ref[...], e_ref[node])
        re, im = g[:RADIX], g[RADIX:]
        out = dot_turned(fourth_ref[...], turn(re * cosine - im * sine, im * cosine + re * sine))
        for c in range(2):
            out_ref[pl.ds(c * nodes + node, RADIX, stride=2 * nodes), :] = out[
                :, c * RADIX : (c + 1) * RADIX
            ]


GRID = (4, 2, 2, 2)


def gathered(share):
    length = share.shape[0]
    if lax.axis_size("freq") != math.prod(GRID):
        return [lax.all_gather(share, "freq", axis=0, tiled=True)], lambda: [[0]]

    def moved(step):
        pairs = []
        for index in np.ndindex(*GRID):
            target = tuple((i + s) % n for i, s, n in zip(index, step, GRID))
            pairs.append((int(np.ravel_multi_index(index, GRID)), int(np.ravel_multi_index(target, GRID))))
        return lambda array: lax.ppermute(array, "freq", pairs)

    own = [(share, [(0, 0, 0, 0)])]
    column = [(moved((d, 0, 0, 0))(share), [(d, 0, 0, 0)]) for d in (1, 2, 3)]
    column = [(jnp.concatenate([a for a, _ in column]), [s for _, ss in column for s in ss])]

    def widened(pieces, steps):
        wide_pieces = list(pieces)
        for step in steps:
            for array, steps_of in pieces:
                wide_pieces.append(
                    (moved(step)(array), [tuple(a + b for a, b in zip(s, step)) for s in steps_of])
                )
        return wide_pieces

    plane = [(0, 0, 1, 0), (0, 1, 0, 0), (0, 1, 1, 0)]
    pieces = widened(widened(own, plane) + widened(column, plane), [(0, 0, 0, 1)])

    def home():
        me = lax.axis_index("freq")
        place = []
        for extent in reversed(GRID):
            place.insert(0, me % extent)
            me = me // extent
        starts = []
        for _, steps in pieces:
            starts.append([])
            for step in steps:
                index = 0
                for at, back, extent in zip(place, step, GRID):
                    index = index * extent + (at - back + extent) % extent
                starts[-1].append(index * length)
        return starts

    return [array for array, _ in pieces], home


def local(mag_field, node_order, source_blocks, impedance):
    devices = lax.axis_size("freq")
    total = node_order.shape[0]
    blocks = total // BSIZE
    slots = BSIZE // devices
    nodes = blocks * slots
    span = mag_field.shape[2]
    rows = NBR * 8 * blocks
    block_shape = (devices, span // RADIX, 2 * nodes, RADIX)
    flat_shape = (RADIX * 2 * nodes, RADIX)
    limit = pltpu.CompilerParams(vmem_limit_bytes=48 << 20)
    first, second, third, fourth, cosine, sine = (jnp.asarray(table) for table in tables())

    pieces, home = gathered(impedance.reshape(rows, -1, RADIX).transpose(1, 0, 2))
    count = devices if len(pieces) > 1 else 1

    outgoing = pl.pallas_call(
        functools.partial(gather_kernel, blocks, slots),
        out_shape=jax.ShapeDtypeStruct(block_shape, jnp.float32),
        in_specs=[VMEM_SPACE] * 2,
        out_specs=VMEM_SPACE,
        compiler_params=limit,
        name="gather_nodes",
    )(node_order.reshape(1, total), mag_field)
    arrived = lax.all_to_all(outgoing, "freq", split_axis=0, concat_axis=0, tiled=True)
    spectrum = pl.pallas_call(
        forward_kernel,
        out_shape=jax.ShapeDtypeStruct((nodes, RADIX, 2 * RADIX), jnp.float32),
        in_specs=[VMEM_SPACE] * 5,
        out_specs=VMEM_SPACE,
        compiler_params=limit,
        name="forward",
    )(arrived.reshape(flat_shape), first, second, cosine, sine)
    field = pl.pallas_call(
        functools.partial(field_kernel, blocks, home),
        out_shape=jax.ShapeDtypeStruct(flat_shape, jnp.float32),
        in_specs=[SMEM_SPACE] + [VMEM_SPACE] * 5 + [pl.BlockSpec(memory_space=pl.ANY)] * len(pieces),
        out_specs=VMEM_SPACE,
        scratch_shapes=[
            pltpu.VMEM((HALF_RADIX, rows, RADIX), jnp.float32),
            pltpu.VMEM((nodes, RADIX, 2 * RADIX), jnp.float32),
            pltpu.SemaphoreType.DMA((count,)),
        ],
        compiler_params=limit,
        name="field",
    )(source_blocks, spectrum, third, fourth, cosine, sine, *pieces)
    returned = lax.all_to_all(
        field.reshape(block_shape), "freq", split_axis=0, concat_axis=0, tiled=True
    )
    return pl.pallas_call(
        functools.partial(scatter_kernel, blocks, slots),
        out_shape=jax.ShapeDtypeStruct((2, total, span), jnp.float32),
        in_specs=[VMEM_SPACE] * 2,
        out_specs=VMEM_SPACE,
        compiler_params=limit,
        name="scatter_nodes",
    )(node_order.reshape(total, 1), returned)


def solution(mesh):
    placed = (
        P(None, "groups", "freq"),
        P("groups"),
        P("groups", None),
        P(None, None, "groups", "freq"),
    )
    return jax.shard_map(
        local, mesh=mesh, in_specs=placed, out_specs=P(None, "groups", "freq"), check_vma=False
    )
```

```python
import functools
import math

import jax
import jax.numpy as jnp
import ml_dtypes
import numpy as np
from jax import lax
from jax.experimental import pallas as pl
from jax.experimental.pallas import tpu as pltpu
from jax.sharding import PartitionSpec as P

RADIX = 128
HALF_RADIX = 64
NT = 16384
BSIZE = 64
NBR = 4
VMEM_SPACE = pl.BlockSpec(memory_space=pltpu.VMEM)
SMEM_SPACE = pl.BlockSpec(memory_space=pltpu.SMEM)
ROW_PAD = 8


def halves(table):
    high = table.astype(ml_dtypes.bfloat16)
    low = (table - high.astype(np.float64)).astype(ml_dtypes.bfloat16)
    return high, low


def wide(table):
    high, low = halves(table)
    return np.concatenate([high, low, high], axis=1)


@functools.cache
def tables():
    full = np.arange(RADIX)
    half = np.arange(HALF_RADIX)

    def wave(rows, cols, modulus):
        theta = 2.0 * math.pi / modulus * (np.outer(rows, cols) % modulus)
        return np.cos(theta), np.sin(theta)

    cos1, sin1 = wave(full, full, RADIX)
    first = np.concatenate([cos1, -sin1], axis=0)
    cos2, sin2 = wave(half, full, RADIX)
    second = np.block([[cos2, sin2], [-sin2, cos2]])
    third = np.block([[cos2.T, -sin2.T], [sin2.T, cos2.T]])
    fourth = np.concatenate([cos1, -sin1], axis=1) * (2.0 / NT)
    twist_cos, twist_sin = wave(full, full, NT)
    return (
        np.stack([wide(first), wide(third)]),
        np.stack([wide(second), wide(fourth)]),
        np.stack([twist_cos, twist_sin]).astype(np.float32),
    )


def two_terms(x):
    high = x.astype(jnp.bfloat16)
    return high, (x - high.astype(jnp.float32)).astype(jnp.bfloat16)


def three_terms(x):
    high = x.astype(jnp.bfloat16)
    rest = x - high.astype(jnp.float32)
    middle = rest.astype(jnp.bfloat16)
    return high, middle, (rest - middle.astype(jnp.float32)).astype(jnp.bfloat16)


def dot_plain(table, x):
    high, low = two_terms(x)
    return jnp.dot(
        table, jnp.concatenate([high, high, low], axis=0), preferred_element_type=jnp.float32
    )


def dot_turned(table, x):
    high, low = two_terms(x)
    return lax.dot_general(
        table,
        jnp.concatenate([high, high, low], axis=1),
        (((1,), (1,)), ((), ())),
        preferred_element_type=jnp.float32,
    )


def slot_of_row(place, blocks, slots):
    device, slot, block = place // (slots * blocks), place // blocks % slots, place % blocks
    return block * BSIZE + device * slots + slot


def gather_kernel(blocks, slots, order_ref, mag_ref, out_ref):
    devices, parts, series, _ = out_ref.shape
    total = order_ref.shape[1]
    nodes = series // 2
    row = lax.broadcasted_iota(jnp.int32, (total, 1), 0)
    wanted = slot_of_row(row, blocks, slots)
    lane = lax.broadcasted_iota(jnp.int32, (total, total), 1)
    node = jnp.sum(
        jnp.where(lane == wanted, order_ref[...], 0).astype(jnp.float32), axis=1, keepdims=True
    ).astype(jnp.int32)
    pick = jnp.where(lane == node, 1.0, 0.0).astype(jnp.bfloat16)
    for c in range(2):
        picked = sum(
            jnp.dot(pick, term, preferred_element_type=jnp.float32)
            for term in three_terms(mag_ref[c])
        )
        for part in range(parts):
            out_ref[:, part, pl.ds(c * nodes, nodes)] = picked[
                :, part * RADIX : (part + 1) * RADIX
            ].reshape(devices, nodes, RADIX)


def scatter_kernel(blocks, slots, order_ref, in_ref, out_ref):
    devices, parts, series, _ = in_ref.shape
    total = order_ref.shape[0]
    nodes = series // 2
    column = lax.broadcasted_iota(jnp.int32, (1, total), 1)
    wanted = slot_of_row(column, blocks, slots)
    place = lax.broadcasted_iota(jnp.int32, (total, total), 0)
    node = jnp.sum(
        jnp.where(place == wanted, order_ref[...], 0).astype(jnp.float32), axis=0, keepdims=True
    ).astype(jnp.int32)
    put = jnp.where(place == node, 1.0, 0.0).astype(jnp.bfloat16)
    for c in range(2):
        value = jnp.concatenate(
            [
                in_ref[:, part, pl.ds(c * nodes, nodes)].reshape(total, RADIX)
                for part in range(parts)
            ],
            axis=1,
        )
        out_ref[c] = sum(
            jnp.dot(put, term, preferred_element_type=jnp.float32) for term in three_terms(value)
        )


def turn(re, im):
    return jnp.concatenate(
        [
            jnp.concatenate([re[:, :RADIX], im[:, :RADIX]], axis=1),
            jnp.concatenate([re[:, RADIX:], im[:, RADIX:]], axis=1),
        ],
        axis=0,
    )


def spread_kernel(impedance_ref, out_ref):
    sources, components, blocks, _ = impedance_ref.shape
    for part in range(out_ref.shape[0]):
        for source in range(sources):
            for component in range(components):
                out_ref[part, pl.ds((source * components + component) * blocks, blocks)] = (
                    impedance_ref[source, component, :, part * RADIX : (part + 1) * RADIX]
                )


def forward_kernel(x_ref, plain_ref, turned_ref, twist_ref, spec_ref):
    nodes = spec_ref.shape[0]
    cosine = jnp.concatenate([twist_ref[0]] * 2, axis=1)
    sine = jnp.concatenate([twist_ref[1]] * 2, axis=1)
    for node in range(nodes):
        x = jnp.concatenate(
            [x_ref[pl.ds(c * nodes + node, RADIX, stride=2 * nodes), :] for c in range(2)], axis=1
        )
        y = dot_plain(plain_ref[0], x)
        re, im = y[:RADIX], y[RADIX:]
        spec_ref[node] = dot_turned(
            turned_ref[0], turn(re * cosine + im * sine, im * cosine - re * sine)
        )


def field_kernel(blocks, home, sources_ref, spec_ref, plain_ref, turned_ref, twist_ref, *refs):
    *piece_refs, out_ref, z_ref, e_ref = refs
    nodes = spec_ref.shape[0]
    slots = nodes // blocks
    pitch = z_ref.shape[1]
    rows = pitch - ROW_PAD
    groups = HALF_RADIX // 8
    for piece_ref, starts in zip(piece_refs, home()):
        length = piece_ref.shape[0] // len(starts)
        for i, start in enumerate(starts):
            z_ref[pl.ds(start, length), pl.ds(0, rows)] = piece_ref[pl.ds(i * length, length)]
    flat = z_ref.reshape(HALF_RADIX * pitch, RADIX)
    first = (lax.broadcasted_iota(jnp.int32, (8, RADIX), 0) == 0) & (
        lax.broadcasted_iota(jnp.int32, (8, RADIX), 1) == 0
    )
    for group in range(groups):
        re_rows = pl.ds(group * 8, 8)
        im_rows = pl.ds(HALF_RADIX + group * 8, 8)
        for block in range(blocks):
            sums = [[0.0] * 4 for _ in range(slots)]
            for source in range(NBR):
                origin = sources_ref[block, source]
                t = [
                    flat[pl.ds(group * 8 * pitch + (source * 8 + i) * blocks + block, 8, stride=pitch), :]
                    for i in range(8)
                ]
                for slot in range(slots):
                    node = slot * blocks + origin
                    bx_re = spec_ref[node, re_rows, :RADIX]
                    by_re = spec_ref[node, re_rows, RADIX:]
                    bx_im = spec_ref[node, im_rows, :RADIX]
                    by_im = spec_ref[node, im_rows, RADIX:]
                    terms = [
                        (t[0] * bx_re - t[1] * bx_im) + (t[2] * by_re - t[3] * by_im),
                        (t[4] * bx_re - t[5] * bx_im) + (t[6] * by_re - t[7] * by_im),
                        (t[0] * bx_im + t[1] * bx_re) + (t[2] * by_im + t[3] * by_re),
                        (t[4] * bx_im + t[5] * bx_re) + (t[6] * by_im + t[7] * by_re),
                    ]
                    sums[slot] = [a + b for a, b in zip(sums[slot], terms)]
            for slot in range(slots):
                node = slot * blocks + block
                values = sums[slot]
                if group == 0:
                    values = [jnp.where(first, 0.0, value) for value in values]
                e_ref[node, re_rows, :RADIX] = values[0]
                e_ref[node, re_rows, RADIX:] = values[1]
                e_ref[node, im_rows, :RADIX] = values[2]
                e_ref[node, im_rows, RADIX:] = values[3]
    cosine = jnp.concatenate([twist_ref[0]] * 2, axis=1)
    sine = jnp.concatenate([twist_ref[1]] * 2, axis=1)
    for node in range(nodes):
        g = dot_plain(plain_ref[1], e_ref[node])
        re, im = g[:RADIX], g[RADIX:]
        out = dot_turned(turned_ref[1], turn(re * cosine - im * sine, im * cosine + re * sine))
        for c in range(2):
            out_ref[pl.ds(c * nodes + node, RADIX, stride=2 * nodes), :] = out[
                :, c * RADIX : (c + 1) * RADIX
            ]


GRID = (4, 2, 2, 2)


def gathered(share):
    length = share.shape[0]
    if lax.axis_size("freq") != math.prod(GRID):
        return [lax.all_gather(share, "freq", axis=0, tiled=True)], lambda: [[0]], share

    def moved(step):
        pairs = []
        for index in np.ndindex(*GRID):
            target = tuple((i + s) % n for i, s, n in zip(index, step, GRID))
            pairs.append((int(np.ravel_multi_index(index, GRID)), int(np.ravel_multi_index(target, GRID))))
        return lambda array: lax.ppermute(array, "freq", pairs)

    def send(piece, step):
        array, steps = piece
        return moved(step)(array), [tuple(a + b for a, b in zip(s, step)) for s in steps]

    def join(*pair):
        return jnp.concatenate([array for array, _ in pair]), [s for _, steps in pair for s in steps]

    along_x, along_y, along_core = (0, 0, 1, 0), (0, 1, 0, 0), (0, 0, 0, 1)

    def over_plane(piece, one, other):
        first = send(piece, one)
        return [piece, first, send(piece, other), send(first, other)]

    own = (share, [(0, 0, 0, 0)])
    up, across, down = (send(own, (d, 0, 0, 0)) for d in (1, 2, 3))
    pieces = (
        over_plane(own, along_y, along_x)
        + over_plane(join(up, across), along_x, along_y)
        + over_plane(down, along_y, along_x)
    )
    pieces = pieces + [send(piece, along_core) for piece in pieces]

    def home():
        me = lax.axis_index("freq")
        place = []
        for extent in reversed(GRID):
            place.insert(0, me % extent)
            me = me // extent
        starts = []
        for _, steps in pieces:
            starts.append([])
            for step in steps:
                index = 0
                for at, back, extent in zip(place, step, GRID):
                    index = index * extent + (at - back + extent) % extent
                starts[-1].append(index * length)
        return starts

    return [array for array, _ in pieces], home, (up[0], across[0], down[0])


def local(mag_field, node_order, source_blocks, impedance):
    devices = lax.axis_size("freq")
    total = node_order.shape[0]
    blocks = total // BSIZE
    slots = BSIZE // devices
    nodes = blocks * slots
    span = mag_field.shape[2]
    rows = NBR * 8 * blocks
    block_shape = (devices, span // RADIX, 2 * nodes, RADIX)
    flat_shape = (RADIX * 2 * nodes, RADIX)
    limit = pltpu.CompilerParams(vmem_limit_bytes=48 << 20)
    plain, turned, twist = (jnp.asarray(table) for table in tables())

    share = pl.pallas_call(
        spread_kernel,
        out_shape=jax.ShapeDtypeStruct((impedance.shape[3] // RADIX, rows, RADIX), jnp.float32),
        in_specs=[VMEM_SPACE],
        out_specs=VMEM_SPACE,
        compiler_params=limit,
        name="spread",
    )(impedance)
    share, mag_field = lax.optimization_barrier((share, mag_field))
    pieces, home, early = gathered(share)

    outgoing = pl.pallas_call(
        functools.partial(gather_kernel, blocks, slots),
        out_shape=jax.ShapeDtypeStruct(block_shape, jnp.float32),
        in_specs=[VMEM_SPACE] * 2,
        out_specs=VMEM_SPACE,
        compiler_params=limit,
        name="gather_nodes",
    )(node_order.reshape(1, total), mag_field)
    outgoing, _ = lax.optimization_barrier((outgoing, early))
    arrived = lax.all_to_all(outgoing, "freq", split_axis=0, concat_axis=0, tiled=True)
    spectrum = pl.pallas_call(
        forward_kernel,
        out_shape=jax.ShapeDtypeStruct((nodes, RADIX, 2 * RADIX), jnp.float32),
        in_specs=[VMEM_SPACE] * 4,
        out_specs=VMEM_SPACE,
        compiler_params=limit,
        name="forward",
    )(arrived.reshape(flat_shape), plain, turned, twist)
    field = pl.pallas_call(
        functools.partial(field_kernel, blocks, home),
        out_shape=jax.ShapeDtypeStruct(flat_shape, jnp.float32),
        in_specs=[SMEM_SPACE] + [VMEM_SPACE] * 4 + [VMEM_SPACE] * len(pieces),
        out_specs=VMEM_SPACE,
        scratch_shapes=[
            pltpu.VMEM((HALF_RADIX, rows + ROW_PAD, RADIX), jnp.float32),
            pltpu.VMEM((nodes, RADIX, 2 * RADIX), jnp.float32),
        ],
        compiler_params=limit,
        name="field",
    )(source_blocks, spectrum, plain, turned, twist, *pieces)
    returned = lax.all_to_all(
        field.reshape(block_shape), "freq", split_axis=0, concat_axis=0, tiled=True
    )
    return pl.pallas_call(
        functools.partial(scatter_kernel, blocks, slots),
        out_shape=jax.ShapeDtypeStruct((2, total, span), jnp.float32),
        in_specs=[VMEM_SPACE] * 2,
        out_specs=VMEM_SPACE,
        compiler_params=limit,
        name="scatter_nodes",
    )(node_order.reshape(total, 1), returned)


def solution(mesh):
    placed = (
        P(None, "groups", "freq"),
        P("groups"),
        P("groups", None),
        P(None, None, "groups", "freq"),
    )
    return jax.shard_map(
        local, mesh=mesh, in_specs=placed, out_specs=P(None, "groups", "freq"), check_vma=False
    )
```

```python
import functools
import math

import jax
import jax.numpy as jnp
import ml_dtypes
import numpy as np
from jax import lax
from jax.experimental import pallas as pl
from jax.experimental.pallas import tpu as pltpu
from jax.sharding import PartitionSpec as P

RADIX = 128
HALF_RADIX = 64
NT = 16384
BSIZE = 64
NBR = 4
HALVES = 1
VMEM_SPACE = pl.BlockSpec(memory_space=pltpu.VMEM)
SMEM_SPACE = pl.BlockSpec(memory_space=pltpu.SMEM)
ROW_PAD = 8


def halves(table):
    high = table.astype(ml_dtypes.bfloat16)
    low = (table - high.astype(np.float64)).astype(ml_dtypes.bfloat16)
    return high, low


def wide(table):
    high, low = halves(table)
    return np.concatenate([high, low, high], axis=1)


@functools.cache
def tables():
    full = np.arange(RADIX)
    half = np.arange(HALF_RADIX)

    def wave(rows, cols, modulus):
        theta = 2.0 * math.pi / modulus * (np.outer(rows, cols) % modulus)
        return np.cos(theta), np.sin(theta)

    cos1, sin1 = wave(full, full, RADIX)
    first = np.concatenate([cos1, -sin1], axis=0)
    cos2, sin2 = wave(half, full, RADIX)
    second = np.block([[cos2, sin2], [-sin2, cos2]])
    third = np.block([[cos2.T, -sin2.T], [sin2.T, cos2.T]])
    fourth = np.concatenate([cos1, -sin1], axis=1) * (2.0 / NT)
    twist_cos, twist_sin = wave(full, full, NT)
    return (
        np.stack([wide(first), wide(third)]),
        np.stack([wide(second), wide(fourth)]),
        np.stack([twist_cos, twist_sin]).astype(np.float32),
    )


def two_terms(x):
    high = x.astype(jnp.bfloat16)
    return high, (x - high.astype(jnp.float32)).astype(jnp.bfloat16)


def three_terms(x):
    high = x.astype(jnp.bfloat16)
    rest = x - high.astype(jnp.float32)
    middle = rest.astype(jnp.bfloat16)
    return high, middle, (rest - middle.astype(jnp.float32)).astype(jnp.bfloat16)


def dot_plain(table, x):
    high, low = two_terms(x)
    return jnp.dot(
        table, jnp.concatenate([high, high, low], axis=0), preferred_element_type=jnp.float32
    )


def dot_turned(table, x):
    high, low = two_terms(x)
    return lax.dot_general(
        table,
        jnp.concatenate([high, high, low], axis=1),
        (((1,), (1,)), ((), ())),
        preferred_element_type=jnp.float32,
    )


def slot_of_row(place, blocks, slots):
    device, slot, block = place // (slots * blocks), place // blocks % slots, place % blocks
    return block * BSIZE + device * slots + slot


def gather_kernel(blocks, slots, order_ref, mag_ref, out_ref):
    devices, parts, series, _ = out_ref.shape
    total = order_ref.shape[1]
    nodes = series // 2
    row = lax.broadcasted_iota(jnp.int32, (total, 1), 0)
    wanted = slot_of_row(row, blocks, slots)
    lane = lax.broadcasted_iota(jnp.int32, (total, total), 1)
    node = jnp.sum(
        jnp.where(lane == wanted, order_ref[...], 0).astype(jnp.float32), axis=1, keepdims=True
    ).astype(jnp.int32)
    pick = jnp.where(lane == node, 1.0, 0.0).astype(jnp.bfloat16)
    for c in range(2):
        picked = sum(
            jnp.dot(pick, term, preferred_element_type=jnp.float32)
            for term in three_terms(mag_ref[c])
        )
        for part in range(parts):
            out_ref[:, part, pl.ds(c * nodes, nodes)] = picked[
                :, part * RADIX : (part + 1) * RADIX
            ].reshape(devices, nodes, RADIX)


def scatter_kernel(blocks, slots, order_ref, in_ref, out_ref):
    devices, parts, series, _ = in_ref.shape
    total = order_ref.shape[0]
    nodes = series // 2
    column = lax.broadcasted_iota(jnp.int32, (1, total), 1)
    wanted = slot_of_row(column, blocks, slots)
    place = lax.broadcasted_iota(jnp.int32, (total, total), 0)
    node = jnp.sum(
        jnp.where(place == wanted, order_ref[...], 0).astype(jnp.float32), axis=0, keepdims=True
    ).astype(jnp.int32)
    put = jnp.where(place == node, 1.0, 0.0).astype(jnp.bfloat16)
    for c in range(2):
        value = jnp.concatenate(
            [
                in_ref[:, part, pl.ds(c * nodes, nodes)].reshape(total, RADIX)
                for part in range(parts)
            ],
            axis=1,
        )
        out_ref[c] = sum(
            jnp.dot(put, term, preferred_element_type=jnp.float32) for term in three_terms(value)
        )


def turn(re, im):
    return jnp.concatenate(
        [
            jnp.concatenate([re[:, :RADIX], im[:, :RADIX]], axis=1),
            jnp.concatenate([re[:, RADIX:], im[:, RADIX:]], axis=1),
        ],
        axis=0,
    )


def spread_kernel(impedance_ref, *out_refs):
    sources, components, blocks, _ = impedance_ref.shape
    few = blocks // HALVES
    for half, out_ref in enumerate(out_refs):
        for part in range(out_ref.shape[0]):
            for source in range(sources):
                for component in range(components):
                    out_ref[part, pl.ds((source * components + component) * few, few)] = impedance_ref[
                        source, component, half * few : (half + 1) * few, part * RADIX : (part + 1) * RADIX
                    ]


def forward_kernel(x_ref, plain_ref, turned_ref, twist_ref, spec_ref):
    nodes = spec_ref.shape[0]
    cosine = jnp.concatenate([twist_ref[0]] * 2, axis=1)
    sine = jnp.concatenate([twist_ref[1]] * 2, axis=1)
    for node in range(nodes):
        x = jnp.concatenate(
            [x_ref[pl.ds(c * nodes + node, RADIX, stride=2 * nodes), :] for c in range(2)], axis=1
        )
        y = dot_plain(plain_ref[0], x)
        re, im = y[:RADIX], y[RADIX:]
        spec_ref[node] = dot_turned(
            turned_ref[0], turn(re * cosine + im * sine, im * cosine - re * sine)
        )


def field_kernel(blocks, homes, sources_ref, spec_ref, plain_ref, turned_ref, twist_ref, *refs):
    *flat_refs, out_ref, z_ref, e_ref = refs
    piece_refs = []
    for home in homes:
        count = len(home())
        piece_refs.append(flat_refs[:count])
        flat_refs = flat_refs[count:]
    nodes = spec_ref.shape[0]
    slots = nodes // blocks
    pitch = z_ref.shape[1]
    few = blocks // HALVES
    rows = NBR * 8 * few
    groups = HALF_RADIX // 8
    for half, home in enumerate(homes):
        for piece_ref, starts in zip(piece_refs[half], home()):
            length = piece_ref.shape[0] // len(starts)
            for i, start in enumerate(starts):
                z_ref[pl.ds(start, length), pl.ds(half * rows, rows)] = piece_ref[
                    pl.ds(i * length, length)
                ]
    flat = z_ref.reshape(HALF_RADIX * pitch, RADIX)
    first = (lax.broadcasted_iota(jnp.int32, (8, RADIX), 0) == 0) & (
        lax.broadcasted_iota(jnp.int32, (8, RADIX), 1) == 0
    )
    for group in range(groups):
        re_rows = pl.ds(group * 8, 8)
        im_rows = pl.ds(HALF_RADIX + group * 8, 8)
        for block in range(blocks):
            sums = [[0.0] * 4 for _ in range(slots)]
            for source in range(NBR):
                origin = sources_ref[block, source]
                base = block // few * rows + block % few
                t = [
                    flat[pl.ds(group * 8 * pitch + base + (source * 8 + i) * few, 8, stride=pitch), :]
                    for i in range(8)
                ]
                for slot in range(slots):
                    node = slot * blocks + origin
                    bx_re = spec_ref[node, re_rows, :RADIX]
                    by_re = spec_ref[node, re_rows, RADIX:]
                    bx_im = spec_ref[node, im_rows, :RADIX]
                    by_im = spec_ref[node, im_rows, RADIX:]
                    terms = [
                        (t[0] * bx_re - t[1] * bx_im) + (t[2] * by_re - t[3] * by_im),
                        (t[4] * bx_re - t[5] * bx_im) + (t[6] * by_re - t[7] * by_im),
                        (t[0] * bx_im + t[1] * bx_re) + (t[2] * by_im + t[3] * by_re),
                        (t[4] * bx_im + t[5] * bx_re) + (t[6] * by_im + t[7] * by_re),
                    ]
                    sums[slot] = [a + b for a, b in zip(sums[slot], terms)]
            for slot in range(slots):
                node = slot * blocks + block
                values = sums[slot]
                if group == 0:
                    values = [jnp.where(first, 0.0, value) for value in values]
                e_ref[node, re_rows, :RADIX] = values[0]
                e_ref[node, re_rows, RADIX:] = values[1]
                e_ref[node, im_rows, :RADIX] = values[2]
                e_ref[node, im_rows, RADIX:] = values[3]
    cosine = jnp.concatenate([twist_ref[0]] * 2, axis=1)
    sine = jnp.concatenate([twist_ref[1]] * 2, axis=1)
    for node in range(nodes):
        g = dot_plain(plain_ref[1], e_ref[node])
        re, im = g[:RADIX], g[RADIX:]
        out = dot_turned(turned_ref[1], turn(re * cosine - im * sine, im * cosine + re * sine))
        for c in range(2):
            out_ref[pl.ds(c * nodes + node, RADIX, stride=2 * nodes), :] = out[
                :, c * RADIX : (c + 1) * RADIX
            ]


GRID = (4, 2, 2, 2)


def gathered(share, by_steps=True):
    length = share.shape[0]
    if not by_steps or lax.axis_size("freq") != math.prod(GRID):
        return [lax.all_gather(share, "freq", axis=0, tiled=True)], lambda: [[0]], share

    def moved(step):
        pairs = []
        for index in np.ndindex(*GRID):
            target = tuple((i + s) % n for i, s, n in zip(index, step, GRID))
            pairs.append((int(np.ravel_multi_index(index, GRID)), int(np.ravel_multi_index(target, GRID))))
        return lambda array: lax.ppermute(array, "freq", pairs)

    def send(piece, step):
        array, steps = piece
        return moved(step)(array), [tuple(a + b for a, b in zip(s, step)) for s in steps]

    own = (share, [(0, 0, 0, 0)])
    plane = ((0, 0, 1, 0), (0, 1, 0, 0), (0, 1, 1, 0))
    column = [send(own, (d, 0, 0, 0)) for d in (1, 2, 3)]
    pieces = [own] + [send(own, step) for step in plane]
    early = [array for array, _ in column + pieces[1:]]
    near = jnp.concatenate(early[:2]), [s for _, steps in column[:2] for s in steps]
    far = column[2]
    near_x, far_y = send(near, plane[0]), send(far, plane[1])
    pieces += [near, near_x, send(near, plane[1]), send(near_x, plane[1])]
    pieces += [far, far_y, send(far, plane[0]), send(far_y, plane[0])]
    pieces = pieces + [send(piece, (0, 0, 0, 1)) for piece in pieces]

    def home():
        me = lax.axis_index("freq")
        place = []
        for extent in reversed(GRID):
            place.insert(0, me % extent)
            me = me // extent
        starts = []
        for _, steps in pieces:
            starts.append([])
            for step in steps:
                index = 0
                for at, back, extent in zip(place, step, GRID):
                    index = index * extent + (at - back + extent) % extent
                starts[-1].append(index * length)
        return starts

    return [array for array, _ in pieces], home, early


def local(mag_field, node_order, source_blocks, impedance):
    devices = lax.axis_size("freq")
    total = node_order.shape[0]
    blocks = total // BSIZE
    slots = BSIZE // devices
    nodes = blocks * slots
    span = mag_field.shape[2]
    rows = NBR * 8 * blocks
    block_shape = (devices, span // RADIX, 2 * nodes, RADIX)
    flat_shape = (RADIX * 2 * nodes, RADIX)
    limit = pltpu.CompilerParams(vmem_limit_bytes=24 << 20)
    plain, turned, twist = (jnp.asarray(table) for table in tables())
    few = blocks // HALVES

    shares = pl.pallas_call(
        spread_kernel,
        out_shape=[
            jax.ShapeDtypeStruct((impedance.shape[3] // RADIX, rows // HALVES, RADIX), jnp.float32)
        ]
        * HALVES,
        in_specs=[VMEM_SPACE],
        out_specs=[VMEM_SPACE] * HALVES,
        compiler_params=limit,
        name="spread",
    )(impedance)
    *shares, mag_field = lax.optimization_barrier((*shares, mag_field))
    tensors = [gathered(share, half == 0) for half, share in enumerate(shares)]
    early = tensors[0][2]
    pieces = [piece for some, _, _ in tensors for piece in some]
    homes = [home for _, home, _ in tensors]

    outgoing = pl.pallas_call(
        functools.partial(gather_kernel, blocks, slots),
        out_shape=jax.ShapeDtypeStruct(block_shape, jnp.float32),
        in_specs=[VMEM_SPACE] * 2,
        out_specs=VMEM_SPACE,
        compiler_params=limit,
        name="gather_nodes",
    )(node_order.reshape(1, total), mag_field)
    outgoing, _ = lax.optimization_barrier((outgoing, early))
    arrived = lax.all_to_all(outgoing, "freq", split_axis=0, concat_axis=0, tiled=True)
    spectrum = pl.pallas_call(
        forward_kernel,
        out_shape=jax.ShapeDtypeStruct((nodes, RADIX, 2 * RADIX), jnp.float32),
        in_specs=[VMEM_SPACE] * 4,
        out_specs=VMEM_SPACE,
        compiler_params=limit,
        name="forward",
    )(arrived.reshape(flat_shape), plain, turned, twist)
    field = pl.pallas_call(
        functools.partial(field_kernel, blocks, homes),
        out_shape=jax.ShapeDtypeStruct(flat_shape, jnp.float32),
        in_specs=[SMEM_SPACE] + [VMEM_SPACE] * (4 + len(pieces)),
        out_specs=VMEM_SPACE,
        scratch_shapes=[
            pltpu.VMEM((HALF_RADIX, rows + ROW_PAD, RADIX), jnp.float32),
            pltpu.VMEM((nodes, RADIX, 2 * RADIX), jnp.float32),
        ],
        compiler_params=limit,
        name="field",
    )(source_blocks, spectrum, plain, turned, twist, *pieces)
    returned = lax.all_to_all(
        field.reshape(block_shape), "freq", split_axis=0, concat_axis=0, tiled=True
    )
    return pl.pallas_call(
        functools.partial(scatter_kernel, blocks, slots),
        out_shape=jax.ShapeDtypeStruct((2, total, span), jnp.float32),
        in_specs=[VMEM_SPACE] * 2,
        out_specs=VMEM_SPACE,
        compiler_params=limit,
        name="scatter_nodes",
    )(node_order.reshape(total, 1), returned)


def solution(mesh):
    placed = (
        P(None, "groups", "freq"),
        P("groups"),
        P("groups", None),
        P(None, None, "groups", "freq"),
    )
    return jax.shard_map(
        local, mesh=mesh, in_specs=placed, out_specs=P(None, "groups", "freq"), check_vma=False
    )
```

```python
import functools
import math

import jax
import jax.numpy as jnp
import ml_dtypes
import numpy as np
from jax import lax
from jax.experimental import pallas as pl
from jax.experimental.pallas import tpu as pltpu
from jax.sharding import PartitionSpec as P

RADIX = 128
HALF_RADIX = 64
NT = 16384
BSIZE = 64
NBR = 4
HALVES = 1
VMEM_SPACE = pl.BlockSpec(memory_space=pltpu.VMEM)
SMEM_SPACE = pl.BlockSpec(memory_space=pltpu.SMEM)
ROW_PAD = 8


def halves(table):
    high = table.astype(ml_dtypes.bfloat16)
    low = (table - high.astype(np.float64)).astype(ml_dtypes.bfloat16)
    return high, low


def wide(table):
    high, low = halves(table)
    return np.concatenate([high, low, high], axis=1)


@functools.cache
def tables():
    full = np.arange(RADIX)
    half = np.arange(HALF_RADIX)

    def wave(rows, cols, modulus):
        theta = 2.0 * math.pi / modulus * (np.outer(rows, cols) % modulus)
        return np.cos(theta), np.sin(theta)

    cos1, sin1 = wave(full, full, RADIX)
    first = np.concatenate([cos1, -sin1], axis=0)
    cos2, sin2 = wave(half, full, RADIX)
    second = np.block([[cos2, sin2], [-sin2, cos2]])
    third = np.block([[cos2.T, -sin2.T], [sin2.T, cos2.T]])
    fourth = np.concatenate([cos1, -sin1], axis=1) * (2.0 / NT)
    twist_cos, twist_sin = wave(full, full, NT)
    return (
        np.stack([wide(first), wide(third)]),
        np.stack([wide(second), wide(fourth)]),
        np.stack([twist_cos, twist_sin]).astype(np.float32),
    )


def two_terms(x):
    high = x.astype(jnp.bfloat16)
    return high, (x - high.astype(jnp.float32)).astype(jnp.bfloat16)


def three_terms(x):
    high = x.astype(jnp.bfloat16)
    rest = x - high.astype(jnp.float32)
    middle = rest.astype(jnp.bfloat16)
    return high, middle, (rest - middle.astype(jnp.float32)).astype(jnp.bfloat16)


def dot_plain(table, x):
    high, low = two_terms(x)
    return jnp.dot(
        table, jnp.concatenate([high, high, low], axis=0), preferred_element_type=jnp.float32
    )


def dot_turned(table, x):
    high, low = two_terms(x)
    return lax.dot_general(
        table,
        jnp.concatenate([high, high, low], axis=1),
        (((1,), (1,)), ((), ())),
        preferred_element_type=jnp.float32,
    )


def slot_of_row(place, blocks, slots):
    device, slot, block = place // (slots * blocks), place // blocks % slots, place % blocks
    return block * BSIZE + device * slots + slot


def gather_kernel(blocks, slots, order_ref, mag_ref, out_ref):
    devices, parts, series, _ = out_ref.shape
    total = order_ref.shape[1]
    nodes = series // 2
    row = lax.broadcasted_iota(jnp.int32, (total, 1), 0)
    wanted = slot_of_row(row, blocks, slots)
    lane = lax.broadcasted_iota(jnp.int32, (total, total), 1)
    node = jnp.sum(
        jnp.where(lane == wanted, order_ref[...], 0).astype(jnp.float32), axis=1, keepdims=True
    ).astype(jnp.int32)
    pick = jnp.where(lane == node, 1.0, 0.0).astype(jnp.bfloat16)
    for c in range(2):
        picked = sum(
            jnp.dot(pick, term, preferred_element_type=jnp.float32)
            for term in three_terms(mag_ref[c])
        )
        for part in range(parts):
            out_ref[:, part, pl.ds(c * nodes, nodes)] = picked[
                :, part * RADIX : (part + 1) * RADIX
            ].reshape(devices, nodes, RADIX)


def scatter_kernel(blocks, slots, order_ref, in_ref, out_ref):
    devices, parts, series, _ = in_ref.shape
    total = order_ref.shape[0]
    nodes = series // 2
    column = lax.broadcasted_iota(jnp.int32, (1, total), 1)
    wanted = slot_of_row(column, blocks, slots)
    place = lax.broadcasted_iota(jnp.int32, (total, total), 0)
    node = jnp.sum(
        jnp.where(place == wanted, order_ref[...], 0).astype(jnp.float32), axis=0, keepdims=True
    ).astype(jnp.int32)
    put = jnp.where(place == node, 1.0, 0.0).astype(jnp.bfloat16)
    for c in range(2):
        value = jnp.concatenate(
            [
                in_ref[:, part, pl.ds(c * nodes, nodes)].reshape(total, RADIX)
                for part in range(parts)
            ],
            axis=1,
        )
        out_ref[c] = sum(
            jnp.dot(put, term, preferred_element_type=jnp.float32) for term in three_terms(value)
        )


def turn(re, im):
    return jnp.concatenate(
        [
            jnp.concatenate([re[:, :RADIX], im[:, :RADIX]], axis=1),
            jnp.concatenate([re[:, RADIX:], im[:, RADIX:]], axis=1),
        ],
        axis=0,
    )


def spread_kernel(impedance_ref, *out_refs):
    sources, components, blocks, _ = impedance_ref.shape
    few = blocks // HALVES
    for half, out_ref in enumerate(out_refs):
        for part in range(out_ref.shape[0]):
            for source in range(sources):
                for component in range(components):
                    out_ref[part, pl.ds((source * components + component) * few, few)] = impedance_ref[
                        source, component, half * few : (half + 1) * few, part * RADIX : (part + 1) * RADIX
                    ]


def forward_kernel(x_ref, plain_ref, turned_ref, twist_ref, spec_ref):
    nodes = spec_ref.shape[0]
    cosine = jnp.concatenate([twist_ref[0]] * 2, axis=1)
    sine = jnp.concatenate([twist_ref[1]] * 2, axis=1)
    for node in range(nodes):
        x = jnp.concatenate(
            [x_ref[pl.ds(c * nodes + node, RADIX, stride=2 * nodes), :] for c in range(2)], axis=1
        )
        y = dot_plain(plain_ref[0], x)
        re, im = y[:RADIX], y[RADIX:]
        spec_ref[node] = dot_turned(
            turned_ref[0], turn(re * cosine + im * sine, im * cosine - re * sine)
        )


def field_kernel(blocks, homes, sources_ref, spec_ref, plain_ref, turned_ref, twist_ref, *refs):
    *flat_refs, out_ref, z_ref, e_ref = refs
    piece_refs = []
    for home in homes:
        count = len(home())
        piece_refs.append(flat_refs[:count])
        flat_refs = flat_refs[count:]
    nodes = spec_ref.shape[0]
    slots = nodes // blocks
    pitch = z_ref.shape[1]
    few = blocks // HALVES
    rows = NBR * 8 * few
    groups = HALF_RADIX // 8
    for half, home in enumerate(homes):
        for piece_ref, starts in zip(piece_refs[half], home()):
            length = piece_ref.shape[0] // len(starts)
            for i, start in enumerate(starts):
                z_ref[pl.ds(start, length), pl.ds(half * rows, rows)] = piece_ref[
                    pl.ds(i * length, length)
                ]
    flat = z_ref.reshape(HALF_RADIX * pitch, RADIX)
    first = (lax.broadcasted_iota(jnp.int32, (8, RADIX), 0) == 0) & (
        lax.broadcasted_iota(jnp.int32, (8, RADIX), 1) == 0
    )
    for group in range(groups):
        re_rows = pl.ds(group * 8, 8)
        im_rows = pl.ds(HALF_RADIX + group * 8, 8)
        for block in range(blocks):
            sums = [[0.0] * 4 for _ in range(slots)]
            for source in range(NBR):
                origin = sources_ref[block, source]
                base = block // few * rows + block % few
                t = [
                    flat[pl.ds(group * 8 * pitch + base + (source * 8 + i) * few, 8, stride=pitch), :]
                    for i in range(8)
                ]
                for slot in range(slots):
                    node = slot * blocks + origin
                    bx_re = spec_ref[node, re_rows, :RADIX]
                    by_re = spec_ref[node, re_rows, RADIX:]
                    bx_im = spec_ref[node, im_rows, :RADIX]
                    by_im = spec_ref[node, im_rows, RADIX:]
                    terms = [
                        (t[0] * bx_re - t[1] * bx_im) + (t[2] * by_re - t[3] * by_im),
                        (t[4] * bx_re - t[5] * bx_im) + (t[6] * by_re - t[7] * by_im),
                        (t[0] * bx_im + t[1] * bx_re) + (t[2] * by_im + t[3] * by_re),
                        (t[4] * bx_im + t[5] * bx_re) + (t[6] * by_im + t[7] * by_re),
                    ]
                    sums[slot] = [a + b for a, b in zip(sums[slot], terms)]
            for slot in range(slots):
                node = slot * blocks + block
                values = sums[slot]
                if group == 0:
                    values = [jnp.where(first, 0.0, value) for value in values]
                e_ref[node, re_rows, :RADIX] = values[0]
                e_ref[node, re_rows, RADIX:] = values[1]
                e_ref[node, im_rows, :RADIX] = values[2]
                e_ref[node, im_rows, RADIX:] = values[3]
    cosine = jnp.concatenate([twist_ref[0]] * 2, axis=1)
    sine = jnp.concatenate([twist_ref[1]] * 2, axis=1)
    for node in range(nodes):
        g = dot_plain(plain_ref[1], e_ref[node])
        re, im = g[:RADIX], g[RADIX:]
        out = dot_turned(turned_ref[1], turn(re * cosine - im * sine, im * cosine + re * sine))
        for c in range(2):
            out_ref[pl.ds(c * nodes + node, RADIX, stride=2 * nodes), :] = out[
                :, c * RADIX : (c + 1) * RADIX
            ]


GRID = (4, 2, 2, 2)


def gathered(share, by_steps=True):
    length = share.shape[0]
    if not by_steps or lax.axis_size("freq") != math.prod(GRID):
        return [lax.all_gather(share, "freq", axis=0, tiled=True)], lambda: [[0]], share

    def moved(step):
        pairs = []
        for index in np.ndindex(*GRID):
            target = tuple((i + s) % n for i, s, n in zip(index, step, GRID))
            pairs.append((int(np.ravel_multi_index(index, GRID)), int(np.ravel_multi_index(target, GRID))))
        return lambda array: lax.ppermute(array, "freq", pairs)

    def send(piece, step):
        array, steps = piece
        return moved(step)(array), [tuple(a + b for a, b in zip(s, step)) for s in steps]

    def join(*some):
        return jnp.concatenate([array for array, _ in some]), [s for _, steps in some for s in steps]

    along_x, along_y, along_core = (0, 0, 1, 0), (0, 1, 0, 0), (0, 0, 0, 1)
    own = (share, [(0, 0, 0, 0)])
    column = [send(own, (d, 0, 0, 0)) for d in (1, 2, 3)]
    beside = [send(own, step) for step in (along_x, along_y, (0, 1, 1, 0))]
    early = [array for array, _ in column + beside]
    near, far = join(*column[:2]), column[2]
    near_x, far_y = send(near, along_x), send(far, along_y)
    near_y, far_x = send(near, along_y), send(far, along_x)
    near_xy, far_yx = send(near_x, along_y), send(far_y, along_x)
    pieces = [join(own, *beside), near, near_x, far, far_x, far_y, near_y, near_xy, far_yx]
    pieces = pieces + [send(piece, along_core) for piece in pieces]

    def home():
        me = lax.axis_index("freq")
        place = []
        for extent in reversed(GRID):
            place.insert(0, me % extent)
            me = me // extent
        starts = []
        for _, steps in pieces:
            starts.append([])
            for step in steps:
                index = 0
                for at, back, extent in zip(place, step, GRID):
                    index = index * extent + (at - back + extent) % extent
                starts[-1].append(index * length)
        return starts

    return [array for array, _ in pieces], home, early


def local(mag_field, node_order, source_blocks, impedance):
    devices = lax.axis_size("freq")
    total = node_order.shape[0]
    blocks = total // BSIZE
    slots = BSIZE // devices
    nodes = blocks * slots
    span = mag_field.shape[2]
    rows = NBR * 8 * blocks
    block_shape = (devices, span // RADIX, 2 * nodes, RADIX)
    flat_shape = (RADIX * 2 * nodes, RADIX)
    limit = pltpu.CompilerParams(vmem_limit_bytes=24 << 20)
    plain, turned, twist = (jnp.asarray(table) for table in tables())
    few = blocks // HALVES

    shares = pl.pallas_call(
        spread_kernel,
        out_shape=[
            jax.ShapeDtypeStruct((impedance.shape[3] // RADIX, rows // HALVES, RADIX), jnp.float32)
        ]
        * HALVES,
        in_specs=[VMEM_SPACE],
        out_specs=[VMEM_SPACE] * HALVES,
        compiler_params=limit,
        name="spread",
    )(impedance)
    *shares, mag_field = lax.optimization_barrier((*shares, mag_field))
    tensors = [gathered(share, half == 0) for half, share in enumerate(shares)]
    early = tensors[0][2]
    pieces = [piece for some, _, _ in tensors for piece in some]
    homes = [home for _, home, _ in tensors]

    outgoing = pl.pallas_call(
        functools.partial(gather_kernel, blocks, slots),
        out_shape=jax.ShapeDtypeStruct(block_shape, jnp.float32),
        in_specs=[VMEM_SPACE] * 2,
        out_specs=VMEM_SPACE,
        compiler_params=limit,
        name="gather_nodes",
    )(node_order.reshape(1, total), mag_field)
    outgoing, _ = lax.optimization_barrier((outgoing, early))
    arrived = lax.all_to_all(outgoing, "freq", split_axis=0, concat_axis=0, tiled=True)
    spectrum = pl.pallas_call(
        forward_kernel,
        out_shape=jax.ShapeDtypeStruct((nodes, RADIX, 2 * RADIX), jnp.float32),
        in_specs=[VMEM_SPACE] * 4,
        out_specs=VMEM_SPACE,
        compiler_params=limit,
        name="forward",
    )(arrived.reshape(flat_shape), plain, turned, twist)
    field = pl.pallas_call(
        functools.partial(field_kernel, blocks, homes),
        out_shape=jax.ShapeDtypeStruct(flat_shape, jnp.float32),
        in_specs=[SMEM_SPACE] + [VMEM_SPACE] * (4 + len(pieces)),
        out_specs=VMEM_SPACE,
        scratch_shapes=[
            pltpu.VMEM((HALF_RADIX, rows + ROW_PAD, RADIX), jnp.float32),
            pltpu.VMEM((nodes, RADIX, 2 * RADIX), jnp.float32),
        ],
        compiler_params=limit,
        name="field",
    )(source_blocks, spectrum, plain, turned, twist, *pieces)
    returned = lax.all_to_all(
        field.reshape(block_shape), "freq", split_axis=0, concat_axis=0, tiled=True
    )
    return pl.pallas_call(
        functools.partial(scatter_kernel, blocks, slots),
        out_shape=jax.ShapeDtypeStruct((2, total, span), jnp.float32),
        in_specs=[VMEM_SPACE] * 2,
        out_specs=VMEM_SPACE,
        compiler_params=limit,
        name="scatter_nodes",
    )(node_order.reshape(total, 1), returned)


def solution(mesh):
    placed = (
        P(None, "groups", "freq"),
        P("groups"),
        P("groups", None),
        P(None, None, "groups", "freq"),
    )
    return jax.shard_map(
        local, mesh=mesh, in_specs=placed, out_specs=P(None, "groups", "freq"), check_vma=False
    )
```

```python
import functools
import math

import jax
import jax.numpy as jnp
import ml_dtypes
import numpy as np
from jax import lax
from jax.experimental import pallas as pl
from jax.experimental.pallas import tpu as pltpu
from jax.sharding import PartitionSpec as P

RADIX = 128
HALF_RADIX = 64
NT = 16384
BSIZE = 64
NBR = 4
VMEM_SPACE = pl.BlockSpec(memory_space=pltpu.VMEM)
SMEM_SPACE = pl.BlockSpec(memory_space=pltpu.SMEM)
ANY_SPACE = pl.BlockSpec(memory_space=pl.ANY)
ROW_PAD = 8


def halves(table):
    high = table.astype(ml_dtypes.bfloat16)
    low = (table - high.astype(np.float64)).astype(ml_dtypes.bfloat16)
    return high, low


def wide(table):
    high, low = halves(table)
    return np.concatenate([high, low, high], axis=1)


@functools.cache
def tables():
    full = np.arange(RADIX)
    half = np.arange(HALF_RADIX)

    def wave(rows, cols, modulus):
        theta = 2.0 * math.pi / modulus * (np.outer(rows, cols) % modulus)
        return np.cos(theta), np.sin(theta)

    cos1, sin1 = wave(full, full, RADIX)
    first = np.concatenate([cos1, -sin1], axis=0)
    cos2, sin2 = wave(half, full, RADIX)
    second = np.block([[cos2, sin2], [-sin2, cos2]])
    third = np.block([[cos2.T, -sin2.T], [sin2.T, cos2.T]])
    fourth = np.concatenate([cos1, -sin1], axis=1) * (2.0 / NT)
    twist_cos, twist_sin = wave(full, full, NT)
    return (
        np.stack([wide(first), wide(third)]),
        np.stack([np.concatenate(halves(second)), np.concatenate(halves(fourth))]),
        np.stack([twist_cos, twist_sin]).astype(np.float32),
    )


def two_terms(x):
    high = x.astype(jnp.bfloat16)
    return high, (x - high.astype(jnp.float32)).astype(jnp.bfloat16)


def three_terms(x):
    high = x.astype(jnp.bfloat16)
    rest = x - high.astype(jnp.float32)
    middle = rest.astype(jnp.bfloat16)
    return high, middle, (rest - middle.astype(jnp.float32)).astype(jnp.bfloat16)


def dot_plain(table, x):
    high, low = two_terms(x)
    return jnp.dot(
        table, jnp.concatenate([high, high, low], axis=0), preferred_element_type=jnp.float32
    )


def dot_turned(table, x):
    high, low = two_terms(x)
    rows = table.shape[0] // 2

    def dot(rows_of, values):
        return lax.dot_general(
            rows_of, values, (((1,), (1,)), ((), ())), preferred_element_type=jnp.float32
        )

    both = dot(table, high)
    return both[:rows] + (both[rows:] + dot(table[:rows], low))


def slot_of_row(place, blocks, slots):
    device, slot, block = place // (slots * blocks), place // blocks % slots, place % blocks
    return block * BSIZE + device * slots + slot


def gather_kernel(blocks, slots, order_ref, mag_ref, out_ref):
    devices, parts, series, _ = out_ref.shape
    total = order_ref.shape[1]
    nodes = series // 2
    row = lax.broadcasted_iota(jnp.int32, (total, 1), 0)
    wanted = slot_of_row(row, blocks, slots)
    lane = lax.broadcasted_iota(jnp.int32, (total, total), 1)
    node = jnp.sum(
        jnp.where(lane == wanted, order_ref[...], 0).astype(jnp.float32), axis=1, keepdims=True
    ).astype(jnp.int32)
    pick = jnp.where(lane == node, 1.0, 0.0).astype(jnp.bfloat16)
    for c in range(2):
        picked = sum(
            jnp.dot(pick, term, preferred_element_type=jnp.float32)
            for term in three_terms(mag_ref[c])
        )
        for part in range(parts):
            out_ref[:, part, pl.ds(c * nodes, nodes)] = picked[
                :, part * RADIX : (part + 1) * RADIX
            ].reshape(devices, nodes, RADIX)


def scatter_kernel(blocks, slots, order_ref, in_ref, out_ref, placed_ref, sems):
    devices, parts, series, _ = in_ref.shape
    total = order_ref.shape[0]
    nodes = series // 2
    column = lax.broadcasted_iota(jnp.int32, (1, total), 1)
    wanted = slot_of_row(column, blocks, slots)
    place = lax.broadcasted_iota(jnp.int32, (total, total), 0)
    node = jnp.sum(
        jnp.where(place == wanted, order_ref[...], 0).astype(jnp.float32), axis=0, keepdims=True
    ).astype(jnp.int32)
    put = jnp.where(place == node, 1.0, 0.0).astype(jnp.bfloat16)
    copies = []
    for c in range(2):
        value = jnp.concatenate(
            [
                in_ref[:, part, pl.ds(c * nodes, nodes)].reshape(total, RADIX)
                for part in range(parts)
            ],
            axis=1,
        )
        placed_ref[c] = sum(
            jnp.dot(put, term, preferred_element_type=jnp.float32) for term in three_terms(value)
        )
        copies.append(pltpu.make_async_copy(placed_ref.at[c], out_ref.at[c], sems.at[c]))
        copies[c].start()
    for copy in copies:
        copy.wait()


def turn(re, im):
    return jnp.concatenate(
        [
            jnp.concatenate([re[:, :RADIX], im[:, :RADIX]], axis=1),
            jnp.concatenate([re[:, RADIX:], im[:, RADIX:]], axis=1),
        ],
        axis=0,
    )


def spread_kernel(impedance_ref, out_ref):
    sources, components, blocks, _ = impedance_ref.shape
    for part in range(out_ref.shape[0]):
        for source in range(sources):
            for component in range(components):
                out_ref[part, pl.ds((source * components + component) * blocks, blocks)] = (
                    impedance_ref[source, component, :, part * RADIX : (part + 1) * RADIX]
                )


def forward_node(x_ref, plain_ref, turned_ref, cosine, sine, spec_ref, node):
    nodes = spec_ref.shape[0]
    x = jnp.concatenate(
        [x_ref[pl.ds(c * nodes + node, RADIX, stride=2 * nodes), :] for c in range(2)], axis=1
    )
    y = dot_plain(plain_ref[0], x)
    re, im = y[:RADIX], y[RADIX:]
    spec_ref[node] = dot_turned(
        turned_ref[0], turn(re * cosine + im * sine, im * cosine - re * sine)
    )


def inverse_node(e_ref, plain_ref, turned_ref, cosine, sine, out_ref, node):
    nodes = e_ref.shape[0]
    g = dot_plain(plain_ref[1], e_ref[node])
    re, im = g[:RADIX], g[RADIX:]
    out = dot_turned(turned_ref[1], turn(re * cosine - im * sine, im * cosine + re * sine))
    for c in range(2):
        out_ref[pl.ds(c * nodes + node, RADIX, stride=2 * nodes), :] = out[
            :, c * RADIX : (c + 1) * RADIX
        ]


def mix_block(blocks, sources_ref, spec_ref, z_ref, e_ref, block):
    slots = spec_ref.shape[0] // blocks
    pitch = z_ref.shape[1]
    flat = z_ref.reshape(HALF_RADIX * pitch, RADIX)
    first = (lax.broadcasted_iota(jnp.int32, (8, RADIX), 0) == 0) & (
        lax.broadcasted_iota(jnp.int32, (8, RADIX), 1) == 0
    )
    for group in range(HALF_RADIX // 8):
        re_rows = pl.ds(group * 8, 8)
        im_rows = pl.ds(HALF_RADIX + group * 8, 8)
        sums = [[0.0] * 4 for _ in range(slots)]
        for source in range(NBR):
            origin = sources_ref[block, source]
            t = [
                flat[pl.ds(group * 8 * pitch + (source * 8 + i) * blocks + block, 8, stride=pitch), :]
                for i in range(8)
            ]
            for slot in range(slots):
                node = slot * blocks + origin
                bx_re = spec_ref[node, re_rows, :RADIX]
                by_re = spec_ref[node, re_rows, RADIX:]
                bx_im = spec_ref[node, im_rows, :RADIX]
                by_im = spec_ref[node, im_rows, RADIX:]
                terms = [
                    (t[0] * bx_re - t[1] * bx_im) + (t[2] * by_re - t[3] * by_im),
                    (t[4] * bx_re - t[5] * bx_im) + (t[6] * by_re - t[7] * by_im),
                    (t[0] * bx_im + t[1] * bx_re) + (t[2] * by_im + t[3] * by_re),
                    (t[4] * bx_im + t[5] * bx_re) + (t[6] * by_im + t[7] * by_re),
                ]
                sums[slot] = [a + b for a, b in zip(sums[slot], terms)]
        for slot in range(slots):
            node = slot * blocks + block
            values = sums[slot]
            if group == 0:
                values = [jnp.where(first, 0.0, value) for value in values]
            e_ref[node, re_rows, :RADIX] = values[0]
            e_ref[node, re_rows, RADIX:] = values[1]
            e_ref[node, im_rows, :RADIX] = values[2]
            e_ref[node, im_rows, RADIX:] = values[3]


def forward_kernel(x_ref, plain_ref, turned_ref, twist_ref, spec_ref):
    cosine = jnp.concatenate([twist_ref[0]] * 2, axis=1)
    sine = jnp.concatenate([twist_ref[1]] * 2, axis=1)
    for node in range(spec_ref.shape[0]):
        forward_node(x_ref, plain_ref, turned_ref, cosine, sine, spec_ref, node)


def field_kernel(blocks, home, sources_ref, spec_ref, plain_ref, turned_ref, twist_ref, *refs):
    *piece_refs, out_ref, z_ref, e_ref = refs
    nodes = e_ref.shape[0]
    rows = z_ref.shape[1] - ROW_PAD
    cosine = jnp.concatenate([twist_ref[0]] * 2, axis=1)
    sine = jnp.concatenate([twist_ref[1]] * 2, axis=1)
    for piece_ref, starts in zip(piece_refs, home()):
        length = piece_ref.shape[0] // len(starts)
        for i, start in enumerate(starts):
            z_ref[pl.ds(start, length), pl.ds(0, rows)] = piece_ref[pl.ds(i * length, length)]
    for block in range(blocks):
        mix_block(blocks, sources_ref, spec_ref, z_ref, e_ref, block)
        for node in range(block, nodes, blocks):
            inverse_node(e_ref, plain_ref, turned_ref, cosine, sine, out_ref, node)


GRID = (4, 2, 2, 2)


def gathered(share):
    length = share.shape[0]
    if lax.axis_size("freq") != math.prod(GRID):
        return [lax.all_gather(share, "freq", axis=0, tiled=True)], lambda: [[0]], share

    def moved(step):
        pairs = []
        for index in np.ndindex(*GRID):
            target = tuple((i + s) % n for i, s, n in zip(index, step, GRID))
            pairs.append((int(np.ravel_multi_index(index, GRID)), int(np.ravel_multi_index(target, GRID))))
        return lambda array: lax.ppermute(array, "freq", pairs)

    def send(piece, step):
        array, steps = piece
        return moved(step)(array), [tuple(a + b for a, b in zip(s, step)) for s in steps]

    def join(*some):
        return jnp.concatenate([array for array, _ in some]), [s for _, steps in some for s in steps]

    along_x, along_y, along_core = (0, 0, 1, 0), (0, 1, 0, 0), (0, 0, 0, 1)
    own = (share, [(0, 0, 0, 0)])
    column = [send(own, (d, 0, 0, 0)) for d in (1, 2, 3)]
    beside = [send(own, step) for step in (along_x, along_y, (0, 1, 1, 0))]
    early = [array for array, _ in column + beside]
    near, far = join(*column[:2]), column[2]
    near_x, far_y = send(near, along_x), send(far, along_y)
    near_y, far_x = send(near, along_y), send(far, along_x)
    near_xy, far_yx = send(near_x, along_y), send(far_y, along_x)
    pieces = [join(own, *beside), near, near_x, far, far_x, far_y, near_y, near_xy, far_yx]
    pieces = pieces + [send(piece, along_core) for piece in pieces]

    def home():
        me = lax.axis_index("freq")
        place = []
        for extent in reversed(GRID):
            place.insert(0, me % extent)
            me = me // extent
        starts = []
        for _, steps in pieces:
            starts.append([])
            for step in steps:
                index = 0
                for at, back, extent in zip(place, step, GRID):
                    index = index * extent + (at - back + extent) % extent
                starts[-1].append(index * length)
        return starts

    return [array for array, _ in pieces], home, early


def local(mag_field, node_order, source_blocks, impedance):
    devices = lax.axis_size("freq")
    total = node_order.shape[0]
    blocks = total // BSIZE
    slots = BSIZE // devices
    nodes = blocks * slots
    span = mag_field.shape[2]
    rows = NBR * 8 * blocks
    block_shape = (devices, span // RADIX, 2 * nodes, RADIX)
    flat_shape = (RADIX * 2 * nodes, RADIX)
    limit = pltpu.CompilerParams(vmem_limit_bytes=24 << 20)
    plain, turned, twist = (jnp.asarray(table) for table in tables())

    share = pl.pallas_call(
        spread_kernel,
        out_shape=jax.ShapeDtypeStruct((impedance.shape[3] // RADIX, rows, RADIX), jnp.float32),
        in_specs=[VMEM_SPACE],
        out_specs=VMEM_SPACE,
        compiler_params=limit,
        name="spread",
    )(impedance)
    share, mag_field = lax.optimization_barrier((share, mag_field))
    pieces, home, early = gathered(share)

    outgoing = pl.pallas_call(
        functools.partial(gather_kernel, blocks, slots),
        out_shape=jax.ShapeDtypeStruct(block_shape, jnp.float32),
        in_specs=[VMEM_SPACE] * 2,
        out_specs=VMEM_SPACE,
        compiler_params=limit,
        name="gather_nodes",
    )(node_order.reshape(1, total), mag_field)
    outgoing, _ = lax.optimization_barrier((outgoing, early))
    arrived = lax.all_to_all(outgoing, "freq", split_axis=0, concat_axis=0, tiled=True)
    spectrum = pl.pallas_call(
        forward_kernel,
        out_shape=jax.ShapeDtypeStruct((nodes, RADIX, 2 * RADIX), jnp.float32),
        in_specs=[VMEM_SPACE] * 4,
        out_specs=VMEM_SPACE,
        compiler_params=limit,
        name="forward",
    )(arrived.reshape(flat_shape), plain, turned, twist)
    field = pl.pallas_call(
        functools.partial(field_kernel, blocks, home),
        out_shape=jax.ShapeDtypeStruct(flat_shape, jnp.float32),
        in_specs=[SMEM_SPACE] + [VMEM_SPACE] * (4 + len(pieces)),
        out_specs=VMEM_SPACE,
        scratch_shapes=[
            pltpu.VMEM((HALF_RADIX, rows + ROW_PAD, RADIX), jnp.float32),
            pltpu.VMEM((nodes, RADIX, 2 * RADIX), jnp.float32),
        ],
        compiler_params=limit,
        name="field",
    )(source_blocks, spectrum, plain, turned, twist, *pieces)
    returned = lax.all_to_all(
        field.reshape(block_shape), "freq", split_axis=0, concat_axis=0, tiled=True
    )
    return pl.pallas_call(
        functools.partial(scatter_kernel, blocks, slots),
        out_shape=jax.ShapeDtypeStruct((2, total, span), jnp.float32),
        in_specs=[VMEM_SPACE] * 2,
        out_specs=ANY_SPACE,
        scratch_shapes=[
            pltpu.VMEM((2, total, span), jnp.float32),
            pltpu.SemaphoreType.DMA((2,)),
        ],
        compiler_params=limit,
        name="scatter_nodes",
    )(node_order.reshape(total, 1), returned)


def solution(mesh):
    placed = (
        P(None, "groups", "freq"),
        P("groups"),
        P("groups", None),
        P(None, None, "groups", "freq"),
    )
    return jax.shard_map(
        local, mesh=mesh, in_specs=placed, out_specs=P(None, "groups", "freq"), check_vma=False
    )
```

```python
import functools
import math

import jax
import jax.numpy as jnp
import ml_dtypes
import numpy as np
from jax import lax
from jax.experimental import pallas as pl
from jax.experimental.pallas import tpu as pltpu
from jax.sharding import PartitionSpec as P

RADIX = 128
HALF_RADIX = 64
NT = 16384
BSIZE = 64
NBR = 4
VMEM_SPACE = pl.BlockSpec(memory_space=pltpu.VMEM)
SMEM_SPACE = pl.BlockSpec(memory_space=pltpu.SMEM)
ANY_SPACE = pl.BlockSpec(memory_space=pl.ANY)
ROW_PAD = 8


def halves(table):
    high = table.astype(ml_dtypes.bfloat16)
    low = (table - high.astype(np.float64)).astype(ml_dtypes.bfloat16)
    return high, low


def wide(table):
    high, low = halves(table)
    return np.concatenate([high, low, high], axis=1)


@functools.cache
def tables():
    full = np.arange(RADIX)
    half = np.arange(HALF_RADIX)

    def wave(rows, cols, modulus):
        theta = 2.0 * math.pi / modulus * (np.outer(rows, cols) % modulus)
        return np.cos(theta), np.sin(theta)

    cos1, sin1 = wave(full, full, RADIX)
    first = np.concatenate([cos1, -sin1], axis=0)
    cos2, sin2 = wave(half, full, RADIX)
    second = np.block([[cos2, sin2], [-sin2, cos2]])
    third = np.block([[cos2.T, -sin2.T], [sin2.T, cos2.T]])
    fourth = np.concatenate([cos1, -sin1], axis=1) * (2.0 / NT)
    twist_cos, twist_sin = wave(full, full, NT)
    return (
        np.stack([wide(first), wide(third)]),
        np.stack([np.concatenate(halves(second)), np.concatenate(halves(fourth))]),
        np.stack([twist_cos, twist_sin]).astype(np.float32),
    )


def two_terms(x):
    high = x.astype(jnp.bfloat16)
    return high, (x - high.astype(jnp.float32)).astype(jnp.bfloat16)


def three_terms(x):
    high = x.astype(jnp.bfloat16)
    rest = x - high.astype(jnp.float32)
    middle = rest.astype(jnp.bfloat16)
    return high, middle, (rest - middle.astype(jnp.float32)).astype(jnp.bfloat16)


def dot_plain(table, x):
    high, low = two_terms(x)
    return jnp.dot(
        table, jnp.concatenate([high, high, low], axis=0), preferred_element_type=jnp.float32
    )


def dot_turned(table, x):
    high, low = two_terms(x)
    rows = table.shape[0] // 2

    def dot(rows_of, values):
        return lax.dot_general(
            rows_of, values, (((1,), (1,)), ((), ())), preferred_element_type=jnp.float32
        )

    both = dot(table, high)
    return both[:rows] + (both[rows:] + dot(table[:rows], low))


def slot_of_row(place, blocks, slots):
    device, slot, block = place // (slots * blocks), place // blocks % slots, place % blocks
    return block * BSIZE + device * slots + slot


def gather_kernel(blocks, slots, order_ref, mag_ref, out_ref):
    devices, parts, series, _ = out_ref.shape
    total = order_ref.shape[1]
    nodes = series // 2
    row = lax.broadcasted_iota(jnp.int32, (total, 1), 0)
    wanted = slot_of_row(row, blocks, slots)
    lane = lax.broadcasted_iota(jnp.int32, (total, total), 1)
    node = jnp.sum(
        jnp.where(lane == wanted, order_ref[...], 0).astype(jnp.float32), axis=1, keepdims=True
    ).astype(jnp.int32)
    pick = jnp.where(lane == node, 1.0, 0.0).astype(jnp.bfloat16)
    for c in range(2):
        picked = sum(
            jnp.dot(pick, term, preferred_element_type=jnp.float32)
            for term in three_terms(mag_ref[c])
        )
        for part in range(parts):
            out_ref[:, part, pl.ds(c * nodes, nodes)] = picked[
                :, part * RADIX : (part + 1) * RADIX
            ].reshape(devices, nodes, RADIX)


def scatter_kernel(blocks, slots, order_ref, in_ref, out_ref, placed_ref, sems):
    devices, parts, series, _ = in_ref.shape
    total = order_ref.shape[0]
    nodes = series // 2
    column = lax.broadcasted_iota(jnp.int32, (1, total), 1)
    wanted = slot_of_row(column, blocks, slots)
    place = lax.broadcasted_iota(jnp.int32, (total, total), 0)
    node = jnp.sum(
        jnp.where(place == wanted, order_ref[...], 0).astype(jnp.float32), axis=0, keepdims=True
    ).astype(jnp.int32)
    put = jnp.where(place == node, 1.0, 0.0).astype(jnp.bfloat16)
    copies = []
    for c in range(2):
        value = jnp.concatenate(
            [
                in_ref[:, part, pl.ds(c * nodes, nodes)].reshape(total, RADIX)
                for part in range(parts)
            ],
            axis=1,
        )
        placed_ref[c] = sum(
            jnp.dot(put, term, preferred_element_type=jnp.float32) for term in three_terms(value)
        )
        copies.append(pltpu.make_async_copy(placed_ref.at[c], out_ref.at[c], sems.at[c]))
        copies[c].start()
    for copy in copies:
        copy.wait()


def turn(re, im):
    return jnp.concatenate(
        [
            jnp.concatenate([re[:, :RADIX], im[:, :RADIX]], axis=1),
            jnp.concatenate([re[:, RADIX:], im[:, RADIX:]], axis=1),
        ],
        axis=0,
    )


def forward_node(x_ref, plain_ref, turned_ref, cosine, sine, spec_ref, node):
    nodes = spec_ref.shape[0]
    x = jnp.concatenate(
        [x_ref[pl.ds(c * nodes + node, RADIX, stride=2 * nodes), :] for c in range(2)], axis=1
    )
    y = dot_plain(plain_ref[0], x)
    re, im = y[:RADIX], y[RADIX:]
    spec_ref[node] = dot_turned(
        turned_ref[0], turn(re * cosine + im * sine, im * cosine - re * sine)
    )


def inverse_node(e_ref, plain_ref, turned_ref, cosine, sine, out_ref, node):
    nodes = e_ref.shape[0]
    g = dot_plain(plain_ref[1], e_ref[node])
    re, im = g[:RADIX], g[RADIX:]
    out = dot_turned(turned_ref[1], turn(re * cosine - im * sine, im * cosine + re * sine))
    for c in range(2):
        out_ref[pl.ds(c * nodes + node, RADIX, stride=2 * nodes), :] = out[
            :, c * RADIX : (c + 1) * RADIX
        ]


def mix_block(blocks, sources_ref, spec_ref, z_ref, e_ref, block):
    slots = spec_ref.shape[0] // blocks
    pitch = z_ref.shape[1]
    flat = z_ref.reshape(HALF_RADIX * pitch, RADIX)
    first = (lax.broadcasted_iota(jnp.int32, (8, RADIX), 0) == 0) & (
        lax.broadcasted_iota(jnp.int32, (8, RADIX), 1) == 0
    )
    for group in range(HALF_RADIX // 8):
        re_rows = pl.ds(group * 8, 8)
        im_rows = pl.ds(HALF_RADIX + group * 8, 8)
        sums = [[0.0] * 4 for _ in range(slots)]
        for source in range(NBR):
            origin = sources_ref[block, source]
            t = [
                flat[pl.ds(group * 8 * pitch + (source * 8 + i) * blocks + block, 8, stride=pitch), :]
                for i in range(8)
            ]
            for slot in range(slots):
                node = slot * blocks + origin
                bx_re = spec_ref[node, re_rows, :RADIX]
                by_re = spec_ref[node, re_rows, RADIX:]
                bx_im = spec_ref[node, im_rows, :RADIX]
                by_im = spec_ref[node, im_rows, RADIX:]
                terms = [
                    (t[0] * bx_re - t[1] * bx_im) + (t[2] * by_re - t[3] * by_im),
                    (t[4] * bx_re - t[5] * bx_im) + (t[6] * by_re - t[7] * by_im),
                    (t[0] * bx_im + t[1] * bx_re) + (t[2] * by_im + t[3] * by_re),
                    (t[4] * bx_im + t[5] * bx_re) + (t[6] * by_im + t[7] * by_re),
                ]
                sums[slot] = [a + b for a, b in zip(sums[slot], terms)]
        for slot in range(slots):
            node = slot * blocks + block
            values = sums[slot]
            if group == 0:
                values = [jnp.where(first, 0.0, value) for value in values]
            e_ref[node, re_rows, :RADIX] = values[0]
            e_ref[node, re_rows, RADIX:] = values[1]
            e_ref[node, im_rows, :RADIX] = values[2]
            e_ref[node, im_rows, RADIX:] = values[3]


def forward_kernel(x_ref, plain_ref, turned_ref, twist_ref, spec_ref):
    cosine = jnp.concatenate([twist_ref[0]] * 2, axis=1)
    sine = jnp.concatenate([twist_ref[1]] * 2, axis=1)
    for node in range(spec_ref.shape[0]):
        forward_node(x_ref, plain_ref, turned_ref, cosine, sine, spec_ref, node)


def field_kernel(blocks, home, sources_ref, spec_ref, plain_ref, turned_ref, twist_ref, *refs):
    *piece_refs, out_ref, z_ref, e_ref = refs
    nodes = e_ref.shape[0]
    cosine = jnp.concatenate([twist_ref[0]] * 2, axis=1)
    sine = jnp.concatenate([twist_ref[1]] * 2, axis=1)
    for piece_ref, starts in zip(piece_refs, home()):
        _, tensors, _, share = piece_ref.shape
        for i, start in enumerate(starts):
            for part in range(share // RADIX):
                for tensor in range(tensors):
                    z_ref[start + part, pl.ds(tensor * blocks, blocks)] = piece_ref[
                        i, tensor, :, part * RADIX : (part + 1) * RADIX
                    ]
    for block in range(blocks):
        mix_block(blocks, sources_ref, spec_ref, z_ref, e_ref, block)
        for node in range(block, nodes, blocks):
            inverse_node(e_ref, plain_ref, turned_ref, cosine, sine, out_ref, node)


GRID = (4, 2, 2, 2)


def gathered(share):
    length = share.shape[3] // RADIX
    devices = lax.axis_size("freq")
    if devices != math.prod(GRID):
        whole = lax.all_gather(share, "freq", axis=0, tiled=True)
        return [whole], lambda: [[i * length for i in range(devices)]], share

    def moved(step):
        pairs = []
        for index in np.ndindex(*GRID):
            target = tuple((i + s) % n for i, s, n in zip(index, step, GRID))
            pairs.append((int(np.ravel_multi_index(index, GRID)), int(np.ravel_multi_index(target, GRID))))
        return lambda array: lax.ppermute(array, "freq", pairs)

    def send(piece, step):
        array, steps = piece
        return moved(step)(array), [tuple(a + b for a, b in zip(s, step)) for s in steps]

    def join(*some):
        return jnp.concatenate([array for array, _ in some]), [s for _, steps in some for s in steps]

    along_x, along_y, along_core = (0, 0, 1, 0), (0, 1, 0, 0), (0, 0, 0, 1)
    own = (share, [(0, 0, 0, 0)])
    column = [send(own, (d, 0, 0, 0)) for d in (1, 2, 3)]
    beside = [send(own, step) for step in (along_x, along_y, (0, 1, 1, 0))]
    early = [array for array, _ in column + beside]
    near, far = join(*column[:2]), column[2]
    near_x, far_y = send(near, along_x), send(far, along_y)
    near_y, far_x = send(near, along_y), send(far, along_x)
    near_xy, far_yx = send(near_x, along_y), send(far_y, along_x)
    pieces = [own, join(*beside), near, near_x, far, far_x, far_y, near_y, near_xy, far_yx]
    pieces = pieces + [send(piece, along_core) for piece in pieces]

    def home():
        me = lax.axis_index("freq")
        place = []
        for extent in reversed(GRID):
            place.insert(0, me % extent)
            me = me // extent
        starts = []
        for _, steps in pieces:
            starts.append([])
            for step in steps:
                index = 0
                for at, back, extent in zip(place, step, GRID):
                    index = index * extent + (at - back + extent) % extent
                starts[-1].append(index * length)
        return starts

    return [array for array, _ in pieces], home, early


def local(mag_field, node_order, source_blocks, impedance):
    devices = lax.axis_size("freq")
    total = node_order.shape[0]
    blocks = total // BSIZE
    slots = BSIZE // devices
    nodes = blocks * slots
    span = mag_field.shape[2]
    rows = NBR * 8 * blocks
    block_shape = (devices, span // RADIX, 2 * nodes, RADIX)
    flat_shape = (RADIX * 2 * nodes, RADIX)
    limit = pltpu.CompilerParams(vmem_limit_bytes=24 << 20)
    plain, turned, twist = (jnp.asarray(table) for table in tables())

    share = impedance.reshape((1, NBR * 8) + impedance.shape[2:])
    pieces, home, early = gathered(share)

    outgoing = pl.pallas_call(
        functools.partial(gather_kernel, blocks, slots),
        out_shape=jax.ShapeDtypeStruct(block_shape, jnp.float32),
        in_specs=[VMEM_SPACE] * 2,
        out_specs=VMEM_SPACE,
        compiler_params=limit,
        name="gather_nodes",
    )(node_order.reshape(1, total), mag_field)
    outgoing, _ = lax.optimization_barrier((outgoing, early))
    arrived = lax.all_to_all(outgoing, "freq", split_axis=0, concat_axis=0, tiled=True)
    spectrum = pl.pallas_call(
        forward_kernel,
        out_shape=jax.ShapeDtypeStruct((nodes, RADIX, 2 * RADIX), jnp.float32),
        in_specs=[VMEM_SPACE] * 4,
        out_specs=VMEM_SPACE,
        compiler_params=limit,
        name="forward",
    )(arrived.reshape(flat_shape), plain, turned, twist)
    field = pl.pallas_call(
        functools.partial(field_kernel, blocks, home),
        out_shape=jax.ShapeDtypeStruct(flat_shape, jnp.float32),
        in_specs=[SMEM_SPACE] + [VMEM_SPACE] * (4 + len(pieces)),
        out_specs=VMEM_SPACE,
        scratch_shapes=[
            pltpu.VMEM((HALF_RADIX, rows + ROW_PAD, RADIX), jnp.float32),
            pltpu.VMEM((nodes, RADIX, 2 * RADIX), jnp.float32),
        ],
        compiler_params=limit,
        name="field",
    )(source_blocks, spectrum, plain, turned, twist, *pieces)
    returned = lax.all_to_all(
        field.reshape(block_shape), "freq", split_axis=0, concat_axis=0, tiled=True
    )
    return pl.pallas_call(
        functools.partial(scatter_kernel, blocks, slots),
        out_shape=jax.ShapeDtypeStruct((2, total, span), jnp.float32),
        in_specs=[VMEM_SPACE] * 2,
        out_specs=ANY_SPACE,
        scratch_shapes=[
            pltpu.VMEM((2, total, span), jnp.float32),
            pltpu.SemaphoreType.DMA((2,)),
        ],
        compiler_params=limit,
        name="scatter_nodes",
    )(node_order.reshape(total, 1), returned)


def solution(mesh):
    placed = (
        P(None, "groups", "freq"),
        P("groups"),
        P("groups", None),
        P(None, None, "groups", "freq"),
    )
    return jax.shard_map(
        local, mesh=mesh, in_specs=placed, out_specs=P(None, "groups", "freq"), check_vma=False
    )
```
